256 devices in a mesh: gx: 8 (over z), gy: 8 (over y, core), gz: 4 (over x).
Axes of the slice: x: 4, y: 4, z: 8, core: 2. Of those that a mesh axis runs over, the one named last changes fastest.
Arguments:
- saved_heat_state: float32 [64, 128, 512], P('gx', 'gy', 'gz'), may hold values from 0 to 1
- forward_motion: float32 [3, 64, 128, 512], P(None, 'gx', 'gy', 'gz'), may hold values from -1 to 1
- dual_heat_after: float32 [64, 128, 512], P('gx', 'gy', 'gz'), may hold values from -1 to 6
- rheology_class: int32 [64, 128, 512], P('gx', 'gy', 'gz'), may hold values from 0 to 7, as said below
- class_base_stiffness: float32 [8], replicated, may hold values from 0.01 to 100
Outputs:
- adj_temp_prev: float32 [64, 128, 512], P('gx', 'gy', 'gz')
- adj_velocity: float32 [3, 64, 128, 512], P(None, 'gx', 'gy', 'gz')
- adj_pressure: float32 [64, 128, 512], P('gx', 'gy', 'gz')
The draws below stay inside these ranges and needn't reach their ends.
Inputs may be any that keep to these rules, and one draw needn't show every extreme that they name: `rheology_class`: each cell's viscosity class.
All inputs are finite; a program needn't handle non-finite values.
Results may differ from the reference program's by a relative error of at most 0.0003.
Values sent between devices are 32-bit elements; how exact they have to be, the bound alone decides.
A program may use at most 128 MiB of HBM per device.

```python
import math
import jax
import jax.numpy as jnp

RECOMPUTE = 2
SCHUR_ITERS = 4
COARSE_SWEEPS = 3
LAYERS = 8
GRID_WIDTH = 64
GRID_BREADTH = 128
GRID_HEIGHT = 512


def draw_saved_heat_state(key, part):
    extent = (GRID_WIDTH, GRID_BREADTH, GRID_HEIGHT)
    uniform_draw = jax.random.uniform(jax.random.fold_in(key, 11), extent, jnp.float32)
    return uniform_draw


def draw_dual_heat_after(key, part):
    extent = (GRID_WIDTH, GRID_BREADTH, GRID_HEIGHT)
    depth_share = jnp.arange(GRID_HEIGHT, dtype=jnp.float32) / GRID_HEIGHT
    rough_part = jnp.clip(jax.random.normal(jax.random.fold_in(key, 22), extent, jnp.float32), -2.5, 2.5)
    offset_part = 1.5 + 2.0 * depth_share
    return offset_part[None, None, :] + rough_part


def draw_rheology_class(key, part):
    extent = (GRID_WIDTH, GRID_BREADTH, GRID_HEIGHT)
    class_order = jax.random.permutation(jax.random.fold_in(key, 31), LAYERS).astype(jnp.int32)
    jitter = jax.random.randint(jax.random.fold_in(key, 32), extent, 0, GRID_HEIGHT // LAYERS, dtype=jnp.int32)
    depth_index = jnp.arange(GRID_HEIGHT, dtype=jnp.int32)[None, None, :]
    depth_band = jnp.minimum((depth_index + jitter) * LAYERS // GRID_HEIGHT, LAYERS - 1)
    return jnp.take(class_order, depth_band).astype(jnp.int32)


def shard_levels(rng, shape, split, smallest, top_value):
    factor_of, own = 1.0, jax.random.fold_in(rng, 6)
    for dim, blocks in split:
        draws = jnp.exp(jax.random.uniform(jax.random.fold_in(own, dim), (blocks,), jnp.float32, smallest / len(split), top_value / len(split)))
        factor_of = factor_of * jnp.repeat(draws, shape[dim] // blocks).reshape([-1 if axis == dim else 1 for axis in range(len(shape))])
    return factor_of


def setup_inputs(seed: int = 0) -> dict:
    streams_of = jax.random.split(jax.random.key(seed), 6)
    saved_heat_state = draw_saved_heat_state(jax.random.fold_in(streams_of[5], 71), 0)
    forward_motion = jnp.clip(jax.random.uniform(streams_of[1], (3, GRID_WIDTH, GRID_BREADTH, GRID_HEIGHT), jnp.float32, -1.0, 1.0) * shard_levels(streams_of[1], (3, GRID_WIDTH, GRID_BREADTH, GRID_HEIGHT), ((1, 8), (2, 8), (3, 4)), -0.4, 0.0), -1.0, 1.0)
    dual_heat_after = draw_dual_heat_after(jax.random.fold_in(streams_of[5], 71), 0)
    rheology_class = draw_rheology_class(jax.random.fold_in(streams_of[5], 71), 0)
    class_base_stiffness = jnp.clip(jnp.exp(jax.random.uniform(streams_of[4], (LAYERS,), jnp.float32, math.log(0.01), math.log(100.0))), 0.01, 100.0)
    return dict(saved_heat_state=saved_heat_state, forward_motion=forward_motion, dual_heat_after=dual_heat_after, rheology_class=rheology_class, class_base_stiffness=class_base_stiffness)


INCREMENT_DT = 0.2
DIFFUSIVITY = 0.3
ACTIVATION_ENERGY = 2.3
JACOBI_WEIGHT = 0.7
SCHUR_WEIGHT = 0.5
RAYLEIGH = 1.0


def widen_boxes(field):
    return jnp.pad(field, [(0, 0)] * (field.ndim - 3) + [(1, 1)] * 3)


def neighbours(bordered_array):
    centre = bordered_array[..., 1:-1, 1:-1, 1:-1]
    beside_all = [bordered_array[..., 2:, 1:-1, 1:-1], bordered_array[..., :-2, 1:-1, 1:-1],
              bordered_array[..., 1:-1, 2:, 1:-1], bordered_array[..., 1:-1, :-2, 1:-1],
              bordered_array[..., 1:-1, 1:-1, 2:], bordered_array[..., 1:-1, 1:-1, :-2]]
    return centre, beside_all


def march_backward(bordered_array, shallower_adjacent, deeper_adjacent):
    centre, beside_all = neighbours(bordered_array)
    drift = 0.0
    for dim_index in range(3):
        drift = drift + shallower_adjacent[dim_index] * (centre - beside_all[2 * dim_index + 1]) + deeper_adjacent[dim_index] * (beside_all[2 * dim_index] - centre)
    spread = sum(beside_all) - 6.0 * centre
    return centre - INCREMENT_DT * drift + INCREMENT_DT * DIFFUSIVITY * spread


def motion_source(bordered_heat, forward_motion, dual_heat_after):
    centre, beside_all = neighbours(bordered_heat)
    device_pieces = [jnp.where(forward_motion[dim_index] > 0, centre - beside_all[2 * dim_index + 1], beside_all[2 * dim_index] - centre) for dim_index in range(3)]
    return -INCREMENT_DT * dual_heat_after[None] * jnp.stack(device_pieces)


def advect_dual_heat(pos_padded, neg_padded, lam_padded):
    centre, beside_all = neighbours(lam_padded)
    result = centre + INCREMENT_DT * DIFFUSIVITY * (sum(beside_all) - 6.0 * centre)
    for dim_index in range(3):
        pos_centre, pos_around = neighbours(pos_padded[dim_index])
        neg_centre, neg_around = neighbours(neg_padded[dim_index])
        result = result - INCREMENT_DT * (pos_centre - pos_around[2 * dim_index] + neg_around[2 * dim_index + 1] - neg_centre)
    return result


def coefficients(bordered_array, factor):
    centre, beside_all = neighbours(bordered_array)
    return [factor * (0.5 * (centre + other)) for other in beside_all]


def apply_operator(face_coef, bordered_array):
    centre, beside_all = neighbours(bordered_array)
    return sum(coef * (centre - other) for coef, other in zip(face_coef, beside_all))


def gradient(bordered_array):
    centre, beside_all = neighbours(bordered_array)
    return jnp.stack([0.5 * (beside_all[2 * dim_index] - beside_all[2 * dim_index + 1]) for dim_index in range(3)])


def divergence(bordered_array):
    centre, beside_all = neighbours(bordered_array)
    return sum(0.5 * (beside_all[2 * dim_index][dim_index] - beside_all[2 * dim_index + 1][dim_index]) for dim_index in range(3))


def restrict(field):
    leading = field.shape[:-3]
    cells_x, cells_y, cells_z = field.shape[-3:]
    blocks = field.reshape(leading + (cells_x // 2, 2, cells_y // 2, 2, cells_z // 2, 2))
    return blocks.mean(axis=(-5, -3, -1))


def prolong(field):
    return jnp.repeat(jnp.repeat(jnp.repeat(field, 2, axis=-3), 2, axis=-2), 2, axis=-1)


def evaluate_viscosity(rheology_class, class_base_stiffness):
    base = jnp.zeros(rheology_class.shape, jnp.float32)
    for layer_index in range(LAYERS):
        base = base + jnp.where(rheology_class == layer_index, class_base_stiffness[layer_index], 0.0)
    return base


def reference(saved_heat_state, forward_motion, dual_heat_after, rheology_class, class_base_stiffness):
    shallower_adjacent = jnp.maximum(forward_motion, 0.0)
    deeper_adjacent = jnp.minimum(forward_motion, 0.0)
    heat_state = saved_heat_state
    for repeat_index in range(RECOMPUTE):
        heat_state = march_backward(widen_boxes(heat_state), shallower_adjacent, deeper_adjacent)
    local_viscosity = evaluate_viscosity(rheology_class, class_base_stiffness) * jnp.exp(-ACTIVATION_ENERGY * heat_state)
    driving_source = motion_source(widen_boxes(heat_state), forward_motion, dual_heat_after)
    advected_result = advect_dual_heat(widen_boxes(shallower_adjacent * dual_heat_after[None]), widen_boxes(deeper_adjacent * dual_heat_after[None]), widen_boxes(dual_heat_after))
    face_coef = coefficients(widen_boxes(local_viscosity), 1.0)
    diagonal = sum(face_coef)
    coarse_coef = coefficients(widen_boxes(restrict(local_viscosity)), 0.25)
    coarse_diag = sum(coarse_coef)
    total_cells = GRID_WIDTH * GRID_BREADTH * GRID_HEIGHT
    velocity = jnp.zeros(forward_motion.shape, jnp.float32)
    mean_stress = jnp.zeros(saved_heat_state.shape, jnp.float32)
    for iteration in range(SCHUR_ITERS):
        if iteration == 0:
            residual = driving_source
        else:
            residual = driving_source - apply_operator(face_coef, widen_boxes(velocity)) - gradient(widen_boxes(mean_stress))
        correction = JACOBI_WEIGHT * residual / diagonal
        residual_two = residual - apply_operator(face_coef, widen_boxes(correction))
        coarse_res = restrict(residual_two)
        coarse_corr = JACOBI_WEIGHT * coarse_res / coarse_diag
        for sweep in range(COARSE_SWEEPS - 1):
            coarse_corr = coarse_corr + JACOBI_WEIGHT * (coarse_res - apply_operator(coarse_coef, widen_boxes(coarse_corr))) / coarse_diag
        correction = correction + prolong(coarse_corr)
        correction = correction + JACOBI_WEIGHT * (residual - apply_operator(face_coef, widen_boxes(correction))) / diagonal
        velocity = velocity + correction
        mean_stress = mean_stress - SCHUR_WEIGHT * local_viscosity * divergence(widen_boxes(velocity))
        mean_stress = mean_stress - jnp.sum(mean_stress) / total_cells
    adj_temp_prev = advected_result + RAYLEIGH * velocity[2]
    return (adj_temp_prev, velocity, mean_stress)
```

```python
import functools

import jax
import jax.numpy as jnp
from jax import lax
from jax.experimental import pallas as pl
from jax.experimental.pallas import tpu as pltpu
from jax.sharding import PartitionSpec as P

RECOMPUTE = 2
SCHUR_ITERS = 4
COARSE_SWEEPS = 3
LAYERS = 8
INCREMENT_DT = 0.2
DIFFUSIVITY = 0.3
ACTIVATION_ENERGY = 2.3
JACOBI_WEIGHT = 0.7
SCHUR_WEIGHT = 0.5
RAYLEIGH = 1.0

MESH = pl.DeviceIdType.MESH
AXES = ("gx", "gy", "gz")
NX, NY, NZ = 8, 16, 128
CX = NX // 2
PITCH = 24
FIRST = 8
KEEP = 1.0 - JACOBI_WEIGHT

HEAT1, HEAT2, FIELDS, PRESSURE, FIRST_SMOOTH, SWEEP1, SWEEP2, LAST_SMOOTH, VELOCITY = range(9)
ROUNDS = 9


def row(plane):
    return FIRST + plane * PITCH


class Item:
    def __init__(self, ref, comps, planes, width, xoff=0, yoff=0, lane=0, first=0):
        self.ref, self.comps, self.planes, self.width = ref, comps, planes, width
        self.xoff, self.yoff, self.lane, self.first = xoff, yoff, lane, first

    def count(self):
        return self.comps * self.planes

    def spot(self, c, x):
        return self.lane + (c * self.planes + x) * 2 * self.width


def kernel(sizes, total_cells, heat, motion, dual, rheology, stiffness, out_t, out_v, out_p, fine, coarse, vel, press,
           fields, cvisc, res, src, adj, held, cres, trans, kf, kc, kh, aux, xs, xr, ys, yr, zs, zr, psum, mean, ar_out,
           ar_in, send_sem, recv_sem, ar_send, ar_recv):
    at = [lax.axis_index(a) for a in AXES]
    barrier = pltpu.get_barrier_semaphore()
    peers = sum(n - 1 for n in sizes)
    for axis, me, n in zip(AXES, at, sizes):
        for d in range(1, n):
            pl.semaphore_signal(barrier, inc=1, device_id={axis: lax.rem(me + d, n)}, device_id_type=MESH)

    lanes = lax.broadcasted_iota(jnp.int32, (NY, NZ), 1)
    rows = lax.broadcasted_iota(jnp.int32, (NY, NZ), 0)
    pair = {1: lanes >> 1, 2: lanes >> 2}
    upper = {1: (lanes & 1) == 1, 2: (lanes & 3) >= 2}
    low = {1: lanes < 1, 2: lanes < 2}
    high = {1: lanes >= NZ - 1, 2: lanes >= NZ - 2}
    even_row = (rows & 1) == 0
    even_lane = (lanes & 1) == 0

    def lroll(v, shift):
        return pltpu.roll(v, shift % NZ, 1)

    def copies(t, xrows, yrows):
        out = []
        for k, (axis, me, n) in enumerate(zip(AXES, at, sizes)):
            for s in (0, 1):
                source = (xs.at[t, s, pl.ds(0, xrows)], ys.at[t, s, pl.ds(0, yrows)], zs.at[t])[k]
                target = (xr.at[t, s, pl.ds(0, xrows)], yr.at[t, s, pl.ds(0, yrows)], zr.at[t, s])[k]
                peer = lax.rem(me + (1 if s == 0 else n - 1), n)
                copy = pltpu.make_async_remote_copy(
                    src_ref=source, dst_ref=target, send_sem=send_sem.at[t, 2 * k + s],
                    recv_sem=recv_sem.at[t, 2 * k + s], device_id={axis: peer}, device_id_type=MESH)
                up, down = me < n - 1, me > 0
                out.append((copy, up if s == 0 else down, down if s == 0 else up))
        return out

    def start(t, xrows, yrows):
        for copy, sends, _ in copies(t, xrows, yrows):
            pl.when(sends)(copy.start)

    def finish(t, xrows, yrows):
        for copy, _, gets in copies(t, xrows, yrows):
            pl.when(gets)(copy.wait_recv)
        for copy, sends, _ in copies(t, xrows, yrows):
            pl.when(sends)(copy.wait_send)

    def pack_lanes(acc, value, spot, w):
        return jnp.where(pair[w] == spot // (2 * w), lroll(value, spot + w), acc)

    def chunks(n):
        return [(a, min(8, n - a)) for a in range(0, n, 8)]

    def pack(t, items):
        acc = jnp.zeros((NY, NZ), jnp.float32)
        for it in items:
            for c in range(it.comps):
                p = (it.first + c) * it.planes
                at_row = it.xoff + c * NY
                xs[t, 0, at_row:at_row + NY] = it.ref[row(p + it.planes - 1):row(p + it.planes - 1) + NY]
                xs[t, 1, at_row:at_row + NY] = it.ref[row(p):row(p) + NY]
            base = row(it.first * it.planes)
            for a, size in chunks(it.count()):
                ys[t, 0, it.yoff + a:it.yoff + a + size] = it.ref[pl.ds(base + a * PITCH + NY - 1, size, stride=PITCH), :]
                ys[t, 1, it.yoff + a:it.yoff + a + size] = it.ref[pl.ds(base + a * PITCH, size, stride=PITCH), :]
            for c in range(it.comps):
                for x in range(it.planes):
                    r = row((it.first + c) * it.planes + x)
                    acc = pack_lanes(acc, it.ref[r:r + NY], it.spot(c, x), it.width)
        zs[t] = acc

    def unpack(t, it, low_extra=None, high_extra=None):
        base = row(it.first * it.planes)
        for a, size in chunks(it.count()):
            below, above = yr[t, 0, it.yoff + a:it.yoff + a + size], yr[t, 1, it.yoff + a:it.yoff + a + size]
            if low_extra is not None:
                below, above = below + low_extra[:size], above + high_extra[:size]
            for k in range(it.width):
                it.ref[pl.ds(base + a * PITCH - 1 - k, size, stride=PITCH), :] = below
                it.ref[pl.ds(base + a * PITCH + NY + k, size, stride=PITCH), :] = above
        return jnp.where(upper[it.width], lroll(zr[t, 0], it.width), lroll(zr[t, 1], -it.width))

    def sides(t, it, c, x):
        r, k = row((it.first + c) * it.planes + x), it.xoff + c * NY
        here = it.ref[r:r + NY]
        xm = xr[t, 0, k:k + NY] if x == 0 else it.ref[r - PITCH:r - PITCH + NY]
        xp = xr[t, 1, k:k + NY] if x == it.planes - 1 else it.ref[r + PITCH:r + PITCH + NY]
        w = it.width
        return here, xm, xp, it.ref[r - w:r - w + NY], it.ref[r + w:r + w + NY]

    def edge(it, c, x, zpairs):
        return lroll(zpairs, -(it.spot(c, x) + it.width))

    def ends(here, at_edge, w):
        return jnp.where(low[w], at_edge, lroll(here, w)), jnp.where(high[w], at_edge, lroll(here, -w))

    def coefs(k, x):
        return [k[n, x * NY:(x + 1) * NY] for n in range(7)]

    def set_coefs(k, x, six, w):
        xm, xp, ym, yp, zm, zp = six
        for n, v in enumerate((xm, xp, ym, yp, jnp.where(low[w], 0.0, zm), jnp.where(high[w], 0.0, zp),
                               jnp.where(low[w], zm, jnp.where(high[w], zp, 0.0)))):
            k[n, x * NY:(x + 1) * NY] = v

    def gather(t, it, c, x, k, zpairs):
        here, xm, xp, ym, yp = sides(t, it, c, x)
        w = it.width
        total = (k[0] * xm + k[1] * xp) + (k[2] * ym + k[3] * yp)
        total = total + (k[4] * lroll(here, w) + k[5] * lroll(here, -w)) + k[6] * edge(it, c, x, zpairs)
        return total, here

    def put(ref, plane, value):
        ref[row(plane):row(plane) + NY] = value

    def get(ref, plane):
        return ref[row(plane):row(plane) + NY]

    def flat(plane):
        return slice(plane * NY, (plane + 1) * NY)

    def restrict_pair(a, b):
        s = a + b
        s = s + jnp.where(even_row, pltpu.roll(s, NY - 1, 0), pltpu.roll(s, 1, 0))
        s = s + jnp.where(even_lane, lroll(s, -1), lroll(s, 1))
        return 0.125 * s

    order = (1, 2, 0)
    base_slot = {}
    slots = 0
    for axis in order:
        base_slot[axis] = slots
        slots += sizes[axis] - 1

    def ar_copies(axis, turn):
        n, me = sizes[axis], at[axis]
        out = []
        for d in range(1, n):
            slot = base_slot[axis] + d - 1
            out.append(pltpu.make_async_remote_copy(
                src_ref=ar_out.at[turn, order.index(axis)], dst_ref=ar_in.at[turn, slot],
                send_sem=ar_send.at[turn, slot], recv_sem=ar_recv.at[turn, slot],
                device_id={AXES[axis]: lax.rem(me + d, n)}, device_id_type=MESH))
        return out

    def ar_start(stage, turn):
        ar_out[turn, stage] = psum[...]
        for copy in ar_copies(order[stage], turn):
            copy.start()

    def ar_finish(stage, turn):
        axis = order[stage]
        pending = ar_copies(axis, turn)
        total = psum[...]
        for copy in pending:
            copy.wait_recv()
        for d in range(1, sizes[axis]):
            total = total + ar_in[turn, base_slot[axis] + d - 1]
        psum[...] = total
        for copy in pending:
            copy.wait_send()

    def put_sum(value):
        s = jnp.sum(jnp.sum(value, axis=0, keepdims=True), axis=1, keepdims=True)
        psum[...] = jnp.broadcast_to(s, (8, NZ))

    def add_mean():
        mean[0] = mean[0] + psum[...]
        mean[1] = mean[1] + (0.5 / total_cells) * mean[0]

    for k, (me, n) in enumerate(zip(at, sizes)):
        for s, gone in ((0, me == 0), (1, me == n - 1)):
            @pl.when(gone)
            def _():
                for t in range(ROUNDS):
                    into = (xr, yr, zr)[k]
                    into[t, s] = jnp.zeros(into.shape[2:], jnp.float32)

    mean[...] = jnp.zeros_like(mean)
    heat_item = Item(fields, 1, NX, 1)
    trans_item = Item(trans, 1, NX, 1, xoff=NY, yoff=NX, lane=2 * NX)
    spread, step = INCREMENT_DT * DIFFUSIVITY, INCREMENT_DT
    for x in range(NX):
        put(fields, x, heat[x])
        lam = dual[x]
        six, total = [], 0.0
        for k in range(3):
            m = motion[k, x]
            am, ap = spread + step * jnp.maximum(m, 0.0), spread - step * jnp.minimum(m, 0.0)
            six += [am, ap]
            total = total + am + ap
        set_coefs(kh, x, six, 1)
        aux[0, flat(x)] = 1.0 - total
        if x == 0:
            xs[HEAT1, 1, NY:2 * NY] = six[0] * lam
        if x == NX - 1:
            xs[HEAT1, 0, NY:2 * NY] = six[1] * lam
        put(trans, x, six[3] * lam)
        put(trans, NX + x, six[2] * lam)
    acc = jnp.zeros((NY, NZ), jnp.float32)
    xs[HEAT1, 0, 0:NY] = heat[NX - 1]
    xs[HEAT1, 1, 0:NY] = heat[0]
    ys[HEAT1, 0, 0:NX] = fields[pl.ds(FIRST + NY - 1, NX, stride=PITCH), :]
    ys[HEAT1, 1, 0:NX] = fields[pl.ds(FIRST, NX, stride=PITCH), :]
    ys[HEAT1, 0, NX:2 * NX] = trans[pl.ds(FIRST + NY - 1, NX, stride=PITCH), :]
    ys[HEAT1, 1, NX:2 * NX] = trans[pl.ds(row(NX), NX, stride=PITCH), :]
    for x in range(NX):
        lam = dual[x]
        acc = pack_lanes(acc, heat[x], heat_item.spot(0, x), 1)
        am = spread + step * jnp.maximum(motion[2, x], 0.0)
        ap = spread - step * jnp.minimum(motion[2, x], 0.0)
        acc = pack_lanes(acc, jnp.where(low[1], am * lam, ap * lam), trans_item.spot(0, x), 1)
    zs[HEAT1] = acc
    pl.semaphore_wait(barrier, peers)
    start(HEAT1, 2 * NY, 2 * NX)
    for x in range(NX):
        base = jnp.zeros((NY, NZ), jnp.float32)
        for layer in range(LAYERS):
            base = jnp.where(rheology[x] == layer, stiffness[layer], base)
        aux[1, flat(x)] = base
    finish(HEAT1, 2 * NY, 2 * NX)

    zpairs = unpack(HEAT1, heat_item)
    stepped = []
    for x in range(NX):
        total, here = gather(HEAT1, heat_item, 0, x, coefs(kh, x), zpairs)
        stepped.append(aux[0, flat(x)] * here + total)
    for x in range(NX):
        put(fields, x, stepped[x])
    pack(HEAT2, [heat_item])
    start(HEAT2, NY, NX)

    for a in (0,):
        trans[pl.ds(row(0) - 1, NX, stride=PITCH), :] = yr[HEAT1, 0, NX:2 * NX]
        trans[pl.ds(row(NX) + NY, NX, stride=PITCH), :] = yr[HEAT1, 1, NX:2 * NX]
    for x in range(NX):
        lam = dual[x]
        ap_x = lambda i: (spread - step * jnp.minimum(motion[0, i], 0.0)) * dual[i]
        am_x = lambda i: (spread + step * jnp.maximum(motion[0, i], 0.0)) * dual[i]
        below = xr[HEAT1, 0, NY:2 * NY] if x == 0 else ap_x(x - 1)
        above = xr[HEAT1, 1, NY:2 * NY] if x == NX - 1 else am_x(x + 1)
        r = row(x)
        total = aux[0, flat(x)] * lam + below + above
        total = total + trans[r - 1:r - 1 + NY] + trans[row(NX + x) + 1:row(NX + x) + 1 + NY]
        am = spread + step * jnp.maximum(motion[2, x], 0.0)
        ap = spread - step * jnp.minimum(motion[2, x], 0.0)
        at_edge = edge(trans_item, 0, x, zpairs)
        total = total + jnp.where(low[1], at_edge, lroll(ap * lam, 1)) + jnp.where(high[1], at_edge, lroll(am * lam, -1))
        out_t[x] = total
    finish(HEAT2, NY, NX)

    zpairs = unpack(HEAT2, heat_item)
    stepped = []
    for x in range(NX):
        total, here = gather(HEAT2, heat_item, 0, x, coefs(kh, x), zpairs)
        stepped.append(aux[0, flat(x)] * here + total)
    for x in range(NX):
        put(fields, x, stepped[x])
        put(fields, NX + x, aux[1, flat(x)] * jnp.exp(-ACTIVATION_ENERGY * stepped[x]))
    for x in range(CX):
        put(cvisc, x, restrict_pair(get(fields, NX + 2 * x), get(fields, NX + 2 * x + 1)))
    both = Item(fields, 2, NX, 1)
    cv_item = Item(cvisc, 1, CX, 2, xoff=2 * NY, yoff=2 * NX, lane=64)
    pack(FIELDS, [both, cv_item])
    start(FIELDS, 3 * NY, 2 * NX + 8)
    finish(FIELDS, 3 * NY, 2 * NX + 8)

    zpairs = unpack(FIELDS, both)
    cpairs = unpack(FIELDS, cv_item)
    for x in range(NX):
        here, xm, xp, ym, yp = sides(FIELDS, both, 0, x)
        zm, zp = ends(here, edge(both, 0, x, zpairs), 1)
        lam = -INCREMENT_DT * dual[x]
        for k, (m, p) in enumerate(((xm, xp), (ym, yp), (zm, zp))):
            src[flat(k * NX + x)] = lam * jnp.where(motion[k, x] > 0, here - m, p - here)
        here, xm, xp, ym, yp = sides(FIELDS, both, 1, x)
        zm, zp = ends(here, edge(both, 1, x, zpairs), 1)
        six = [0.5 * (here + v) for v in (xm, xp, ym, yp, zm, zp)]
        set_coefs(kf, x, six, 1)
        diagonal = (six[0] + six[1]) + (six[2] + six[3]) + (six[4] + six[5])
        inverse = JACOBI_WEIGHT / diagonal
        aux[2, flat(x)] = diagonal
        aux[3, flat(x)] = inverse
        aux[4, flat(x)] = (0.5 * SCHUR_WEIGHT) * here
        for k, (m, p) in enumerate(((xm, xp), (ym, yp), (zm, zp))):
            g = 0.5 * (p - m)
            s = src[flat(k * NX + x)]
            res[flat((3 + k) * NX + x)] = g
            res[flat(k * NX + x)] = s
            put(fine, (3 + k) * NX + x, inverse * g)
            put(fine, k * NX + x, inverse * s)
    for x in range(CX):
        here, xm, xp, ym, yp = sides(FIELDS, cv_item, 0, x)
        zm, zp = ends(here, edge(cv_item, 0, x, cpairs), 2)
        six = [0.125 * (here + v) for v in (xm, xp, ym, yp, zm, zp)]
        set_coefs(kc, x, six, 2)
        aux[5, flat(x)] = JACOBI_WEIGHT / ((six[0] + six[1]) + (six[2] + six[3]) + (six[4] + six[5]))

    def cycle(nc, during, first):
        fi, ci = Item(fine, nc, NX, 1), Item(coarse, nc, CX, 2)
        fx, fy, cx, cy = nc * NY, nc * NX, nc * NY, (nc * CX + 7) // 8 * 8
        pack(FIRST_SMOOTH, [fi])
        start(FIRST_SMOOTH, fx, fy)
        during(0)
        finish(FIRST_SMOOTH, fx, fy)
        zpairs = unpack(FIRST_SMOOTH, fi)
        for x in range(CX):
            inv_c = aux[5, flat(x)]
            ka, kb = coefs(kf, 2 * x), coefs(kf, 2 * x + 1)
            for c in range(nc):
                pa, pb = c * NX + 2 * x, c * NX + 2 * x + 1
                a = KEEP * res[flat(pa)] + gather(FIRST_SMOOTH, fi, c, 2 * x, ka, zpairs)[0]
                b = KEEP * res[flat(pb)] + gather(FIRST_SMOOTH, fi, c, 2 * x + 1, kb, zpairs)[0]
                if first and c >= 3:
                    held[flat(pa - 3 * NX)] = a
                    held[flat(pb - 3 * NX)] = b
                r = restrict_pair(a, b)
                cres[flat(c * CX + x)] = r
                put(coarse, c * CX + x, inv_c * r)
        for sweep in range(COARSE_SWEEPS - 1):
            t = SWEEP1 + sweep
            pack(t, [ci])
            start(t, cx, cy)
            during(1 + sweep)
            finish(t, cx, cy)
            cpairs = unpack(t, ci)
            last = sweep == COARSE_SWEEPS - 2
            swept = []
            for x in range(CX):
                inv_c = aux[5, flat(x)]
                k = coefs(kc, x)
                for c in range(nc):
                    total, here = gather(t, ci, c, x, k, cpairs)
                    e = KEEP * here + inv_c * (cres[flat(c * CX + x)] + total)
                    if last:
                        for q in (2 * x, 2 * x + 1):
                            put(fine, c * NX + q, get(fine, c * NX + q) + e)
                    else:
                        swept.append((c * CX + x, e))
            for plane, e in swept:
                put(coarse, plane, e)
        pack(LAST_SMOOTH, [fi])
        start(LAST_SMOOTH, fx, fy)
        during(3)
        finish(LAST_SMOOTH, fx, fy)
        zpairs = unpack(LAST_SMOOTH, fi)
        for x in range(NX):
            k = coefs(kf, x)
            inverse = aux[3, flat(x)]
            for c in range(nc):
                total, here = gather(LAST_SMOOTH, fi, c, x, k, zpairs)
                new = KEEP * here + inverse * (res[flat(c * NX + x)] + total)
                if c >= 3:
                    adj[flat((c - 3) * NX + x)] = new
                elif first:
                    put(vel, c * NX + x, new)
                else:
                    put(vel, c * NX + x, get(vel, c * NX + x) + new)

    vel_item, press_item = Item(vel, 3, NX, 1), Item(press, 1, NX, 1)

    def divergence(during, first):
        pack(VELOCITY, [vel_item])
        start(VELOCITY, 3 * NY, 3 * NX)
        during()
        finish(VELOCITY, 3 * NY, 3 * NX)
        zpairs = unpack(VELOCITY, vel_item)
        for x in range(NX):
            _, xm, xp, _, _ = sides(VELOCITY, vel_item, 0, x)
            _, _, _, ym, yp = sides(VELOCITY, vel_item, 1, x)
            here = get(vel, 2 * NX + x)
            zm, zp = ends(here, edge(vel_item, 2, x, zpairs), 1)
            change = aux[4, flat(x)] * ((xp - xm) + (yp - ym) + (zp - zm))
            put(press, x, -change if first else get(press, x) - change)

    def first_during(stage):
        if stage == 3:
            acc = jnp.zeros((NY, NZ), jnp.float32)
            for x in range(NX):
                inverse = aux[3, flat(x)]
                for c in range(3):
                    p = c * NX + x
                    acc = acc + held[flat(p)] * get(fine, p)
                    acc = acc + (inverse * res[flat(3 * NX + p)]) * res[flat(p)]
            put_sum(acc)
            ar_start(0, 0)

    cycle(6, first_during, True)

    def first_sum():
        ar_finish(0, 0)
        ar_start(1, 0)

    divergence(first_sum, True)
    ar_finish(1, 0)
    ar_start(2, 0)

    lowest = [jnp.where(me == 0, 1.0, 0.0) for me in at]
    highest = [jnp.where(me == n - 1, 1.0, 0.0) for me, n in zip(at, sizes)]

    def iteration(turn, carry):
        pack(PRESSURE, [press_item])
        start(PRESSURE, NY, NX)
        zpairs = jnp.where(upper[1], lroll(zr[VELOCITY, 0], 1), lroll(zr[VELOCITY, 1], -1))
        for x in range(NX):
            k = coefs(kf, x)
            diagonal = aux[2, flat(x)]
            for c in range(3):
                total, here = gather(VELOCITY, vel_item, c, x, k, zpairs)
                res[flat(c * NX + x)] = src[flat(c * NX + x)] - diagonal * here + total
        finish(PRESSURE, NY, NX)
        ar_finish(2, turn - 1)
        add_mean()
        m8 = mean[1]
        m = jnp.concatenate([m8, m8], axis=0)
        zpairs = unpack(PRESSURE, press_item, lowest[1] * m8, highest[1] * m8)
        zfill = jnp.where(low[1], lowest[2], highest[2]) * m
        for x in range(NX):
            inverse = aux[3, flat(x)]
            here, xm, xp, ym, yp = sides(PRESSURE, press_item, 0, x)
            if x == 0:
                xm = xm + lowest[0] * m
            if x == NX - 1:
                xp = xp + highest[0] * m
            zm, zp = ends(here, edge(press_item, 0, x, zpairs) + zfill, 1)
            for c, (a, b) in enumerate(((xm, xp), (ym, yp), (zm, zp))):
                r = res[flat(c * NX + x)] - 0.5 * (b - a)
                res[flat(c * NX + x)] = r
                put(fine, c * NX + x, inverse * r)

        def during(stage):
            if stage == 0:
                acc = jnp.zeros((NY, NZ), jnp.float32)
                for p in range(3 * NX):
                    acc = acc + adj[flat(p)] * res[flat(p)]
                put_sum(acc)
                ar_start(0, turn)
            elif stage == 1:
                ar_finish(0, turn)
                ar_start(1, turn)
            elif stage == 2:
                ar_finish(1, turn)
                ar_start(2, turn)

        cycle(3, during, False)
        divergence(lambda: None, False)
        return carry

    lax.fori_loop(1, SCHUR_ITERS, iteration, 0)

    ar_finish(2, SCHUR_ITERS - 1)
    add_mean()
    m8 = mean[1]
    m = jnp.concatenate([m8, m8], axis=0)
    for x in range(NX):
        out_p[x] = get(press, x) - m
        for c in range(3):
            out_v[c, x] = get(vel, c * NX + x)
        out_t[x] = out_t[x] + RAYLEIGH * get(vel, 2 * NX + x)


def solution(mesh):
    sizes = tuple(mesh.shape[a] for a in AXES)

    def shards(heat, motion, dual, rheology, stiffness):
        cells = heat.size * sizes[0] * sizes[1] * sizes[2]
        vmem = pl.BlockSpec(memory_space=pltpu.VMEM)
        f32 = jnp.float32
        padded = lambda planes: pltpu.VMEM((FIRST + planes * PITCH, NZ), f32)
        flat = lambda planes: pltpu.VMEM((planes * NY, NZ), f32)
        slots = sum(n - 1 for n in sizes)
        return pl.pallas_call(
            functools.partial(kernel, sizes, cells),
            out_shape=(
                jax.ShapeDtypeStruct(heat.shape, f32),
                jax.ShapeDtypeStruct(motion.shape, f32),
                jax.ShapeDtypeStruct(heat.shape, f32),
            ),
            in_specs=[vmem] * 4 + [pl.BlockSpec(memory_space=pltpu.SMEM)],
            out_specs=(vmem,) * 3,
            scratch_shapes=[
                padded(6 * NX), padded(6 * CX), padded(3 * NX), padded(NX), padded(2 * NX), padded(CX),
                flat(6 * NX), flat(3 * NX), flat(3 * NX), flat(3 * NX), flat(6 * CX), padded(2 * NX),
                pltpu.VMEM((7, NX * NY, NZ), f32), pltpu.VMEM((7, CX * NY, NZ), f32), pltpu.VMEM((7, NX * NY, NZ), f32),
                pltpu.VMEM((6, NX * NY, NZ), f32),
                pltpu.VMEM((ROUNDS, 2, 6 * NY, NZ), f32), pltpu.VMEM((ROUNDS, 2, 6 * NY, NZ), f32),
                pltpu.VMEM((ROUNDS, 2, 6 * NX, NZ), f32), pltpu.VMEM((ROUNDS, 2, 6 * NX, NZ), f32),
                pltpu.VMEM((ROUNDS, NY, NZ), f32), pltpu.VMEM((ROUNDS, 2, NY, NZ), f32),
                pltpu.VMEM((8, NZ), f32), pltpu.VMEM((2, 8, NZ), f32),
                pltpu.VMEM((SCHUR_ITERS, 3, 8, NZ), f32), pltpu.VMEM((SCHUR_ITERS, slots, 8, NZ), f32),
                pltpu.SemaphoreType.DMA((ROUNDS, 6)), pltpu.SemaphoreType.DMA((ROUNDS, 6)),
                pltpu.SemaphoreType.DMA((SCHUR_ITERS, slots)), pltpu.SemaphoreType.DMA((SCHUR_ITERS, slots)),
            ],
            compiler_params=pltpu.CompilerParams(collective_id=0, has_side_effects=True),
        )(heat, motion, dual, rheology, stiffness)

    return jax.shard_map(
        shards,
        mesh=mesh,
        in_specs=(P(*AXES), P(None, *AXES), P(*AXES), P(*AXES), P()),
        out_specs=(P(*AXES), P(None, *AXES), P(*AXES)),
        check_vma=False,
    )
```

```python
import functools

import jax
import jax.numpy as jnp
from jax import lax
from jax.experimental import pallas as pl
from jax.experimental.pallas import tpu as pltpu
from jax.sharding import PartitionSpec as P

RECOMPUTE = 2
SCHUR_ITERS = 4
COARSE_SWEEPS = 3
LAYERS = 8
INCREMENT_DT = 0.2
DIFFUSIVITY = 0.3
ACTIVATION_ENERGY = 2.3
JACOBI_WEIGHT = 0.7
SCHUR_WEIGHT = 0.5
RAYLEIGH = 1.0

MESH = pl.DeviceIdType.MESH
AXES = ("gx", "gy", "gz")
NX, NY, NZ = 8, 16, 128
CX = NX // 2
PITCH = 24
FIRST = 8
KEEP = 1.0 - JACOBI_WEIGHT

HEAT1, HEAT2, FIELDS, PRESSURE, FIRST_SMOOTH, VELOCITY = range(6)
ROUNDS = 6

CY, CZ = NY // 2, NZ // 2
DEPTH = COARSE_SWEEPS
EX = CX + 2 * DEPTH
ER = 16
COARSE_VISC, COARSE_ITERATE = range(2)
AROUND = [(dx, dy, dz) for dx in (-1, 0, 1) for dy in (-1, 0, 1) for dz in (-1, 0, 1) if (dx, dy, dz) != (0, 0, 0)]


def row(plane):
    return FIRST + plane * PITCH


class Item:
    def __init__(self, ref, comps, planes, width, xoff=0, yoff=0, lane=0, first=0):
        self.ref, self.comps, self.planes, self.width = ref, comps, planes, width
        self.xoff, self.yoff, self.lane, self.first = xoff, yoff, lane, first

    def count(self):
        return self.comps * self.planes

    def spot(self, c, x):
        return self.lane + (c * self.planes + x) * 2 * self.width


def kernel(sizes, total_cells, heat, motion, dual, rheology, stiffness, out_t, out_v, out_p, fine, vel, press,
           fields, res, src, adj, held, trans, kf, kc, kh, aux, xs, xr, ys, yr, zs, zr, psum, mean, ar_out, ar_in,
           own, wide, swept, halves, grown, grown_ends, cinv, cxs, cys, czs, czys, cxr, cyr, cxyr, czr, czyr, zq,
           send_sem, recv_sem, ar_send, ar_recv, c_send, c_recv):
    at = [lax.axis_index(a) for a in AXES]
    barrier = pltpu.get_barrier_semaphore()
    peers = sum(n - 1 for n in sizes)
    for axis, me, n in zip(AXES, at, sizes):
        for d in range(1, n):
            pl.semaphore_signal(barrier, inc=1, device_id={axis: lax.rem(me + d, n)}, device_id_type=MESH)

    def there(d):
        ok = None
        for me, n, step in zip(at, sizes, d):
            if step:
                inside = me < n - 1 if step > 0 else me > 0
                ok = inside if ok is None else jnp.logical_and(ok, inside)
        return ok

    def device(d):
        return {axis: lax.rem(me + n + step, n) for axis, me, n, step in zip(AXES, at, sizes, d)}

    for d in AROUND:
        if sum(map(abs, d)) > 1:
            @pl.when(there(d))
            def _():
                pl.semaphore_signal(barrier, inc=1, device_id=device(d), device_id_type=MESH)
            peers = peers + there(d).astype(jnp.int32)

    lanes = lax.broadcasted_iota(jnp.int32, (NY, NZ), 1)
    rows = lax.broadcasted_iota(jnp.int32, (NY, NZ), 0)
    pair = {1: lanes >> 1, 2: lanes >> 2}
    upper = {1: (lanes & 1) == 1, 2: (lanes & 3) >= 2}
    low = {1: lanes < 1, 2: lanes < 2}
    high = {1: lanes >= NZ - 1, 2: lanes >= NZ - 2}
    even_row = (rows & 1) == 0
    even_lane = (lanes & 1) == 0

    def lroll(v, shift):
        return pltpu.roll(v, shift % NZ, 1)

    def copies(t, xrows, yrows):
        out = []
        for k, (axis, me, n) in enumerate(zip(AXES, at, sizes)):
            for s in (0, 1):
                source = (xs.at[t, s, pl.ds(0, xrows)], ys.at[t, s, pl.ds(0, yrows)], zs.at[t])[k]
                target = (xr.at[t, s, pl.ds(0, xrows)], yr.at[t, s, pl.ds(0, yrows)], zr.at[t, s])[k]
                peer = lax.rem(me + (1 if s == 0 else n - 1), n)
                copy = pltpu.make_async_remote_copy(
                    src_ref=source, dst_ref=target, send_sem=send_sem.at[t, 2 * k + s],
                    recv_sem=recv_sem.at[t, 2 * k + s], device_id={axis: peer}, device_id_type=MESH)
                up, down = me < n - 1, me > 0
                out.append((copy, up if s == 0 else down, down if s == 0 else up))
        return out

    def start(t, xrows, yrows):
        for copy, sends, _ in copies(t, xrows, yrows):
            pl.when(sends)(copy.start)

    def finish(t, xrows, yrows):
        for copy, _, gets in copies(t, xrows, yrows):
            pl.when(gets)(copy.wait_recv)
        for copy, sends, _ in copies(t, xrows, yrows):
            pl.when(sends)(copy.wait_send)

    def pack_lanes(acc, value, spot, w):
        return jnp.where(pair[w] == spot // (2 * w), lroll(value, spot + w), acc)

    def chunks(n):
        return [(a, min(8, n - a)) for a in range(0, n, 8)]

    def pack(t, items):
        acc = jnp.zeros((NY, NZ), jnp.float32)
        for it in items:
            for c in range(it.comps):
                p = (it.first + c) * it.planes
                at_row = it.xoff + c * NY
                xs[t, 0, at_row:at_row + NY] = it.ref[row(p + it.planes - 1):row(p + it.planes - 1) + NY]
                xs[t, 1, at_row:at_row + NY] = it.ref[row(p):row(p) + NY]
            base = row(it.first * it.planes)
            for a, size in chunks(it.count()):
                ys[t, 0, it.yoff + a:it.yoff + a + size] = it.ref[pl.ds(base + a * PITCH + NY - 1, size, stride=PITCH), :]
                ys[t, 1, it.yoff + a:it.yoff + a + size] = it.ref[pl.ds(base + a * PITCH, size, stride=PITCH), :]
            for c in range(it.comps):
                for x in range(it.planes):
                    r = row((it.first + c) * it.planes + x)
                    acc = pack_lanes(acc, it.ref[r:r + NY], it.spot(c, x), it.width)
        zs[t] = acc

    def unpack(t, it, low_extra=None, high_extra=None):
        base = row(it.first * it.planes)
        for a, size in chunks(it.count()):
            below, above = yr[t, 0, it.yoff + a:it.yoff + a + size], yr[t, 1, it.yoff + a:it.yoff + a + size]
            if low_extra is not None:
                below, above = below + low_extra[:size], above + high_extra[:size]
            for k in range(it.width):
                it.ref[pl.ds(base + a * PITCH - 1 - k, size, stride=PITCH), :] = below
                it.ref[pl.ds(base + a * PITCH + NY + k, size, stride=PITCH), :] = above
        return jnp.where(upper[it.width], lroll(zr[t, 0], it.width), lroll(zr[t, 1], -it.width))

    def sides(t, it, c, x):
        r, k = row((it.first + c) * it.planes + x), it.xoff + c * NY
        here = it.ref[r:r + NY]
        xm = xr[t, 0, k:k + NY] if x == 0 else it.ref[r - PITCH:r - PITCH + NY]
        xp = xr[t, 1, k:k + NY] if x == it.planes - 1 else it.ref[r + PITCH:r + PITCH + NY]
        w = it.width
        return here, xm, xp, it.ref[r - w:r - w + NY], it.ref[r + w:r + w + NY]

    def edge(it, c, x, zpairs):
        return lroll(zpairs, -(it.spot(c, x) + it.width))

    def ends(here, at_edge, w):
        return jnp.where(low[w], at_edge, lroll(here, w)), jnp.where(high[w], at_edge, lroll(here, -w))

    def coefs(k, x):
        return [k[n, x * NY:(x + 1) * NY] for n in range(7)]

    def set_coefs(k, x, six, w):
        xm, xp, ym, yp, zm, zp = six
        for n, v in enumerate((xm, xp, ym, yp, jnp.where(low[w], 0.0, zm), jnp.where(high[w], 0.0, zp),
                               jnp.where(low[w], zm, jnp.where(high[w], zp, 0.0)))):
            k[n, x * NY:(x + 1) * NY] = v

    def gather(t, it, c, x, k, zpairs):
        here, xm, xp, ym, yp = sides(t, it, c, x)
        w = it.width
        total = (k[0] * xm + k[1] * xp) + (k[2] * ym + k[3] * yp)
        total = total + (k[4] * lroll(here, w) + k[5] * lroll(here, -w)) + k[6] * edge(it, c, x, zpairs)
        return total, here

    def put(ref, plane, value):
        ref[row(plane):row(plane) + NY] = value

    def get(ref, plane):
        return ref[row(plane):row(plane) + NY]

    def flat(plane):
        return slice(plane * NY, (plane + 1) * NY)

    lanes8 = lax.broadcasted_iota(jnp.int32, (CY, NZ), 1)
    left8 = lanes8 < CZ
    left = lanes < CZ
    left4 = lax.broadcasted_iota(jnp.int32, (4, NZ), 1) < CZ
    squeeze = 2 * (lanes8 & (CZ - 1))
    repeat = lanes >> 1
    outer = jnp.where(lanes == 0, NZ - 1, CZ)
    beyond = jnp.where(lanes >= NZ - DEPTH, lanes - (NZ - DEPTH), (lanes - CZ + DEPTH) & 7)

    def take(v, index):
        return jnp.take_along_axis(v, index, axis=1)

    def tile(p):
        return slice(p * CY, (p + 1) * CY)

    def restrict(slot, a, b):
        r = slot * NY
        halves[r:r + NY] = a + b
        t = halves[pl.ds(r, CY, stride=2), :] + halves[pl.ds(r + 1, CY, stride=2), :]
        return take(t + lroll(t, -1), squeeze) * 0.125

    def c_copies(t, nc):
        xr_n, yr_n, z_n = (3 * nc + 1) // 2 * CY, 8 * nc, (CX * nc + 15) // 16 * CY
        out = []
        for i, d in enumerate(AROUND):
            dx, dy, dz = d
            hx, hy, hz = (dx < 0) * 1, (dy < 0) * 1, (dz < 0) * 1
            if dz:
                if dy:
                    source = czys.at[t, hy, pl.ds(0, z_n // 2)]
                    target = czyr.at[t, dx + 1, hy, hz, pl.ds(0, z_n // 2)]
                else:
                    source, target = czs.at[t, pl.ds(0, z_n)], czr.at[t, dx + 1, hz, pl.ds(0, z_n)]
            elif dx and dy:
                source = cys.at[t, hy, pl.ds(0 if dx < 0 else 4 * nc, 4 * nc)]
                target = cxyr.at[t, hx, hy, pl.ds(0, 4 * nc)]
            elif dy:
                source, target = cys.at[t, hy, pl.ds(0, yr_n)], cyr.at[t, hy, pl.ds(0, yr_n)]
            else:
                source, target = cxs.at[t, hx, pl.ds(0, xr_n)], cxr.at[t, hx, pl.ds(0, xr_n)]
            copy = pltpu.make_async_remote_copy(
                src_ref=source, dst_ref=target, send_sem=c_send.at[t, i], recv_sem=c_recv.at[t, i],
                device_id=device(d), device_id_type=MESH)
            out.append((copy, there(d), there(tuple(-v for v in d))))
        return out

    def c_start(t, nc):
        for h, first in ((0, 1), (1, 0)):
            for q in range((3 * nc + 1) // 2):
                a, b = first * nc + 2 * q, first * nc + min(2 * q + 1, 3 * nc - 1)
                cxs[t, h, tile(q)] = jnp.where(left8, own[tile(a)], own[tile(b)])
            rows_from = 4 if h == 0 else 0
            for q in range(2 * nc):
                a, b = 2 * q * CY + rows_from, (2 * q + 1) * CY + rows_from
                cys[t, h, 4 * q:4 * q + 4] = jnp.where(left4, own[a:a + 4], own[b:b + 4])
        for part in range((CX * nc + 15) // 16):
            acc = jnp.zeros((CY, NZ), jnp.float32)
            for g in range(16 * part, min(16 * part + 16, CX * nc)):
                spot = g % 16 * 8
                acc = jnp.where((lanes8 >> 3) == g % 16, lroll(own[tile(g)], spot - (CZ - DEPTH)), acc)
            czs[t, tile(part)] = acc
            czys[t, 0, 4 * part:4 * part + 4] = acc[4:8]
            czys[t, 1, 4 * part:4 * part + 4] = acc[0:4]
        for copy, sends, _ in c_copies(t, nc):
            pl.when(sends)(copy.start)

    def c_finish(t, nc):
        for copy, _, gets in c_copies(t, nc):
            pl.when(gets)(copy.wait_recv)
        for copy, sends, _ in c_copies(t, nc):
            pl.when(sends)(copy.wait_send)

    def wide_row(c, e):
        return FIRST + (c * EX + e) * ER

    def assemble(t, nc):
        group = (lanes8 & 7) < DEPTH
        group4 = (lax.broadcasted_iota(jnp.int32, (4, NZ), 1) & 7) < DEPTH
        for dx in range(3):
            for part in range((CX * nc + 15) // 16):
                r = (dx * 2 + part) * ER
                zq[r + 4:r + 12] = jnp.where(group, czr[t, dx, 0, tile(part)], czr[t, dx, 1, tile(part)])
                for h, at_row in ((0, 0), (1, 12)):
                    four = slice(4 * part, 4 * part + 4)
                    zq[r + at_row:r + at_row + 4] = jnp.where(group4, czyr[t, dx, h, 0, four], czyr[t, dx, h, 1, four])
        for c in range(nc):
            for e in range(EX):
                x = e - DEPTH
                r = wide_row(c, e)
                if 0 <= x < CX:
                    dx, sender = 0, x
                elif x < 0:
                    dx, sender = -1, x + CX
                else:
                    dx, sender = 1, x - CX
                p = sender * nc + c
                if dx == 0:
                    wide[r + 4:r + 12] = own[tile(p)]
                else:
                    i = p - (nc if dx < 0 else 0)
                    v = cxr[t, 0 if dx < 0 else 1, tile(i // 2)]
                    wide[r + 4:r + 12] = v if i % 2 == 0 else lroll(v, CZ)
                if -DEPTH < x < CX + DEPTH - 1:
                    q = p // 2
                    for h, at_row in ((0, 0), (1, 12)):
                        if dx == 0:
                            v = cyr[t, h, 4 * q:4 * q + 4]
                        else:
                            k = 4 * (q - (nc if dx < 0 else 0))
                            v = cxyr[t, 0 if dx < 0 else 1, h, k:k + 4]
                        wide[r + at_row:r + at_row + 4] = v if p % 2 == 0 else lroll(v, CZ)
                    g = p
                    z = zq[((dx_from(dx)) * 2 + g // 16) * ER:((dx_from(dx)) * 2 + g // 16) * ER + ER]
                    wide[r:r + ER] = jnp.where(left, wide[r:r + ER], take(z, (beyond + g % 16 * 8) & (NZ - 1)))

    def dx_from(dx):
        return 1 - dx

    def sweep(source, target, c, e, keep):
        r = wide_row(c, e)
        k = [kc[n, e * ER:(e + 1) * ER] for n in range(6)]
        here = source[r:r + ER]
        total = keep * here + k[0] * source[r - ER:r] + k[1] * source[r + ER:r + 2 * ER]
        total = total + k[2] * source[r - 1:r - 1 + ER] + k[3] * source[r + 1:r + 1 + ER]
        return total + k[4] * lroll(here, 1) + k[5] * lroll(here, -1)

    order = (1, 2, 0)
    base_slot = {}
    slots = 0
    for axis in order:
        base_slot[axis] = slots
        slots += sizes[axis] - 1

    def ar_copies(axis, turn):
        n, me = sizes[axis], at[axis]
        out = []
        for d in range(1, n):
            slot = base_slot[axis] + d - 1
            out.append(pltpu.make_async_remote_copy(
                src_ref=ar_out.at[turn, order.index(axis)], dst_ref=ar_in.at[turn, slot],
                send_sem=ar_send.at[turn, slot], recv_sem=ar_recv.at[turn, slot],
                device_id={AXES[axis]: lax.rem(me + d, n)}, device_id_type=MESH))
        return out

    def ar_start(stage, turn):
        ar_out[turn, stage] = psum[...]
        for copy in ar_copies(order[stage], turn):
            copy.start()

    def ar_finish(stage, turn):
        axis = order[stage]
        pending = ar_copies(axis, turn)
        total = psum[...]
        for copy in pending:
            copy.wait_recv()
        for d in range(1, sizes[axis]):
            total = total + ar_in[turn, base_slot[axis] + d - 1]
        psum[...] = total
        for copy in pending:
            copy.wait_send()

    def put_sum(value):
        s = jnp.sum(jnp.sum(value, axis=0, keepdims=True), axis=1, keepdims=True)
        psum[...] = jnp.broadcast_to(s, (8, NZ))

    def add_mean():
        mean[0] = mean[0] + psum[...]
        mean[1] = mean[1] + (0.5 / total_cells) * mean[0]

    for k, (me, n) in enumerate(zip(at, sizes)):
        for s, gone in ((0, me == 0), (1, me == n - 1)):
            @pl.when(gone)
            def _():
                for t in range(ROUNDS):
                    into = (xr, yr, zr)[k]
                    into[t, s] = jnp.zeros(into.shape[2:], jnp.float32)

    for d in AROUND:
        @pl.when(jnp.logical_not(there(tuple(-v for v in d))))
        def _():
            dx, dy, dz = d
            hx, hy, hz = (dx < 0) * 1, (dy < 0) * 1, (dz < 0) * 1
            for t in range(2):
                if dz and dy:
                    into = czyr.at[t, dx + 1, hy, hz]
                elif dz:
                    into = czr.at[t, dx + 1, hz]
                elif dx and dy:
                    into = cxyr.at[t, hx, hy]
                elif dy:
                    into = cyr.at[t, hy]
                else:
                    into = cxr.at[t, hx]
                into[...] = jnp.zeros(into.shape, jnp.float32)

    wide[...] = jnp.zeros_like(wide)
    mean[...] = jnp.zeros_like(mean)
    heat_item = Item(fields, 1, NX, 1)
    trans_item = Item(trans, 1, NX, 1, xoff=NY, yoff=NX, lane=2 * NX)
    spread, step = INCREMENT_DT * DIFFUSIVITY, INCREMENT_DT
    for x in range(NX):
        put(fields, x, heat[x])
        lam = dual[x]
        six, total = [], 0.0
        for k in range(3):
            m = motion[k, x]
            am, ap = spread + step * jnp.maximum(m, 0.0), spread - step * jnp.minimum(m, 0.0)
            six += [am, ap]
            total = total + am + ap
        set_coefs(kh, x, six, 1)
        aux[0, flat(x)] = 1.0 - total
        if x == 0:
            xs[HEAT1, 1, NY:2 * NY] = six[0] * lam
        if x == NX - 1:
            xs[HEAT1, 0, NY:2 * NY] = six[1] * lam
        put(trans, x, six[3] * lam)
        put(trans, NX + x, six[2] * lam)
    acc = jnp.zeros((NY, NZ), jnp.float32)
    xs[HEAT1, 0, 0:NY] = heat[NX - 1]
    xs[HEAT1, 1, 0:NY] = heat[0]
    ys[HEAT1, 0, 0:NX] = fields[pl.ds(FIRST + NY - 1, NX, stride=PITCH), :]
    ys[HEAT1, 1, 0:NX] = fields[pl.ds(FIRST, NX, stride=PITCH), :]
    ys[HEAT1, 0, NX:2 * NX] = trans[pl.ds(FIRST + NY - 1, NX, stride=PITCH), :]
    ys[HEAT1, 1, NX:2 * NX] = trans[pl.ds(row(NX), NX, stride=PITCH), :]
    for x in range(NX):
        lam = dual[x]
        acc = pack_lanes(acc, heat[x], heat_item.spot(0, x), 1)
        am = spread + step * jnp.maximum(motion[2, x], 0.0)
        ap = spread - step * jnp.minimum(motion[2, x], 0.0)
        acc = pack_lanes(acc, jnp.where(low[1], am * lam, ap * lam), trans_item.spot(0, x), 1)
    zs[HEAT1] = acc
    pl.semaphore_wait(barrier, peers)
    start(HEAT1, 2 * NY, 2 * NX)
    for x in range(NX):
        base = jnp.zeros((NY, NZ), jnp.float32)
        for layer in range(LAYERS):
            base = jnp.where(rheology[x] == layer, stiffness[layer], base)
        aux[1, flat(x)] = base
    finish(HEAT1, 2 * NY, 2 * NX)

    zpairs = unpack(HEAT1, heat_item)
    stepped = []
    for x in range(NX):
        total, here = gather(HEAT1, heat_item, 0, x, coefs(kh, x), zpairs)
        stepped.append(aux[0, flat(x)] * here + total)
    for x in range(NX):
        put(fields, x, stepped[x])
    pack(HEAT2, [heat_item])
    start(HEAT2, NY, NX)

    for a in (0,):
        trans[pl.ds(row(0) - 1, NX, stride=PITCH), :] = yr[HEAT1, 0, NX:2 * NX]
        trans[pl.ds(row(NX) + NY, NX, stride=PITCH), :] = yr[HEAT1, 1, NX:2 * NX]
    for x in range(NX):
        lam = dual[x]
        ap_x = lambda i: (spread - step * jnp.minimum(motion[0, i], 0.0)) * dual[i]
        am_x = lambda i: (spread + step * jnp.maximum(motion[0, i], 0.0)) * dual[i]
        below = xr[HEAT1, 0, NY:2 * NY] if x == 0 else ap_x(x - 1)
        above = xr[HEAT1, 1, NY:2 * NY] if x == NX - 1 else am_x(x + 1)
        r = row(x)
        total = aux[0, flat(x)] * lam + below + above
        total = total + trans[r - 1:r - 1 + NY] + trans[row(NX + x) + 1:row(NX + x) + 1 + NY]
        am = spread + step * jnp.maximum(motion[2, x], 0.0)
        ap = spread - step * jnp.minimum(motion[2, x], 0.0)
        at_edge = edge(trans_item, 0, x, zpairs)
        total = total + jnp.where(low[1], at_edge, lroll(ap * lam, 1)) + jnp.where(high[1], at_edge, lroll(am * lam, -1))
        out_t[x] = total
    finish(HEAT2, NY, NX)

    zpairs = unpack(HEAT2, heat_item)
    stepped = []
    for x in range(NX):
        total, here = gather(HEAT2, heat_item, 0, x, coefs(kh, x), zpairs)
        stepped.append(aux[0, flat(x)] * here + total)
    for x in range(NX):
        put(fields, x, stepped[x])
        put(fields, NX + x, aux[1, flat(x)] * jnp.exp(-ACTIVATION_ENERGY * stepped[x]))
    for x in range(CX):
        own[tile(x)] = restrict(x, get(fields, NX + 2 * x), get(fields, NX + 2 * x + 1))
    both = Item(fields, 2, NX, 1)
    c_start(COARSE_VISC, 1)
    pack(FIELDS, [both])
    start(FIELDS, 2 * NY, 2 * NX)
    finish(FIELDS, 2 * NY, 2 * NX)

    zpairs = unpack(FIELDS, both)
    for x in range(NX):
        here, xm, xp, ym, yp = sides(FIELDS, both, 0, x)
        zm, zp = ends(here, edge(both, 0, x, zpairs), 1)
        lam = -INCREMENT_DT * dual[x]
        for k, (m, p) in enumerate(((xm, xp), (ym, yp), (zm, zp))):
            src[flat(k * NX + x)] = lam * jnp.where(motion[k, x] > 0, here - m, p - here)
        here, xm, xp, ym, yp = sides(FIELDS, both, 1, x)
        zm, zp = ends(here, edge(both, 1, x, zpairs), 1)
        six = [0.5 * (here + v) for v in (xm, xp, ym, yp, zm, zp)]
        set_coefs(kf, x, six, 1)
        diagonal = (six[0] + six[1]) + (six[2] + six[3]) + (six[4] + six[5])
        inverse = JACOBI_WEIGHT / diagonal
        aux[2, flat(x)] = diagonal
        aux[3, flat(x)] = inverse
        aux[4, flat(x)] = (0.5 * SCHUR_WEIGHT) * here
        for k, (m, p) in enumerate(((xm, xp), (ym, yp), (zm, zp))):
            g = 0.5 * (p - m)
            s = src[flat(k * NX + x)]
            res[flat((3 + k) * NX + x)] = g
            res[flat(k * NX + x)] = s
            put(fine, (3 + k) * NX + x, inverse * g)
            put(fine, k * NX + x, inverse * s)
    c_finish(COARSE_VISC, 1)
    assemble(COARSE_VISC, 1)
    inside_rows = jnp.logical_and(jnp.logical_or(rows >= 4, at[1] > 0), jnp.logical_or(rows < 12, at[1] < sizes[1] - 1))
    inside = jnp.logical_or(left, jnp.logical_or(
        jnp.logical_and(lanes >= NZ - DEPTH, at[2] > 0),
        jnp.logical_and(lanes < CZ + DEPTH, at[2] < sizes[2] - 1)))
    inside = jnp.logical_and(inside, inside_rows)
    for e in range(1, EX - 1):
        r = wide_row(0, e)
        here = wide[r:r + ER]
        others = (wide[r - ER:r], wide[r + ER:r + 2 * ER], wide[r - 1:r - 1 + ER], wide[r + 1:r + 1 + ER],
                  lroll(here, 1), lroll(here, -1))
        six = [0.125 * (here + v) for v in others]
        ok = inside
        if e < DEPTH:
            ok = jnp.logical_and(ok, at[0] > 0)
        elif e >= DEPTH + CX:
            ok = jnp.logical_and(ok, at[0] < sizes[0] - 1)
        inverse = jnp.where(ok, JACOBI_WEIGHT / ((six[0] + six[1]) + (six[2] + six[3]) + (six[4] + six[5])), 0.0)
        for n in range(6):
            kc[n, e * ER:(e + 1) * ER] = jnp.where(ok, inverse * six[n], 0.0)
        if DEPTH <= e < DEPTH + CX:
            grown[0:ER] = inverse
            cinv[tile(e - DEPTH)] = take(grown[4:12], lanes8 & (CZ - 1))

    def cycle(nc, during, first):
        fi = Item(fine, nc, NX, 1)
        fx, fy = nc * NY, nc * NX
        pack(FIRST_SMOOTH, [fi])
        start(FIRST_SMOOTH, fx, fy)
        during(0)
        finish(FIRST_SMOOTH, fx, fy)
        zpairs = unpack(FIRST_SMOOTH, fi)
        for x in range(CX):
            ka, kb = coefs(kf, 2 * x), coefs(kf, 2 * x + 1)
            for c in range(nc):
                pa, pb = c * NX + 2 * x, c * NX + 2 * x + 1
                a = KEEP * res[flat(pa)] + gather(FIRST_SMOOTH, fi, c, 2 * x, ka, zpairs)[0]
                b = KEEP * res[flat(pb)] + gather(FIRST_SMOOTH, fi, c, 2 * x + 1, kb, zpairs)[0]
                if first and c >= 3:
                    held[flat(pa - 3 * NX)] = a
                    held[flat(pb - 3 * NX)] = b
                own[tile(x * nc + c)] = cinv[tile(x)] * restrict(x * nc + c, a, b)
        c_start(COARSE_ITERATE, nc)
        during(1)
        c_finish(COARSE_ITERATE, nc)
        assemble(COARSE_ITERATE, nc)
        for e in range(1, EX - 1):
            for c in range(nc):
                r = wide_row(c, e)
                swept[r:r + ER] = sweep(wide, swept, c, e, 2.0 - JACOBI_WEIGHT)
        for e in range(2, EX - 2):
            for c in range(nc):
                r = wide_row(c, e)
                v = wide[r:r + ER] + sweep(swept, None, c, e, KEEP)
                base = (c * 6 + e - 2) * 2 * ER
                full = take(v, repeat)
                for k in (0, 8):
                    for odd in (0, 1):
                        grown[pl.ds(base + 2 * k + odd, 8, stride=2), :] = full[k:k + 8]
                if DEPTH <= e < DEPTH + CX:
                    base = (c * CX + e - DEPTH) * 2 * ER
                    full = take(v, outer)
                    for k in (0, 8):
                        for odd in (0, 1):
                            grown_ends[pl.ds(base + 2 * k + odd, 8, stride=2), :] = full[k:k + 8]

        acc = jnp.zeros((NY, NZ), jnp.float32)
        for x in range(NX):
            k = coefs(kf, x)
            inverse = aux[3, flat(x)]
            for c in range(nc):
                here, xm, xp, ym, yp = sides(FIRST_SMOOTH, fi, c, x)
                base = [(c * 6 + q // 2 + 1) * 2 * ER + FIRST for q in (x - 1, x, x + 1)]
                whole = here + grown[base[1]:base[1] + NY]
                total = k[0] * (xm + grown[base[0]:base[0] + NY]) + k[1] * (xp + grown[base[2]:base[2] + NY])
                total = total + k[2] * (ym + grown[base[1] - 1:base[1] - 1 + NY])
                total = total + k[3] * (yp + grown[base[1] + 1:base[1] + 1 + NY])
                at_edge = (c * CX + x // 2) * 2 * ER + FIRST
                total = total + k[4] * lroll(whole, 1) + k[5] * lroll(whole, -1)
                total = total + k[6] * (edge(fi, c, x, zpairs) + grown_ends[at_edge:at_edge + NY])
                new = KEEP * whole + here + inverse * total
                if c >= 3:
                    adj[flat((c - 3) * NX + x)] = new
                elif first:
                    put(vel, c * NX + x, new)
                    p = c * NX + x
                    acc = acc + held[flat(p)] * whole + get(fine, 3 * NX + p) * res[flat(p)]
                else:
                    put(vel, c * NX + x, get(vel, c * NX + x) + new)
        if first:
            put_sum(acc)
            ar_start(0, 0)

    vel_item, press_item = Item(vel, 3, NX, 1), Item(press, 1, NX, 1)

    def divergence(during, first):
        pack(VELOCITY, [vel_item])
        start(VELOCITY, 3 * NY, 3 * NX)
        during()
        finish(VELOCITY, 3 * NY, 3 * NX)
        zpairs = unpack(VELOCITY, vel_item)
        for x in range(NX):
            _, xm, xp, _, _ = sides(VELOCITY, vel_item, 0, x)
            _, _, _, ym, yp = sides(VELOCITY, vel_item, 1, x)
            here = get(vel, 2 * NX + x)
            zm, zp = ends(here, edge(vel_item, 2, x, zpairs), 1)
            change = aux[4, flat(x)] * ((xp - xm) + (yp - ym) + (zp - zm))
            put(press, x, -change if first else get(press, x) - change)

    cycle(6, lambda stage: None, True)

    def first_sum():
        ar_finish(0, 0)
        ar_start(1, 0)

    divergence(first_sum, True)
    ar_finish(1, 0)
    ar_start(2, 0)

    lowest = [jnp.where(me == 0, 1.0, 0.0) for me in at]
    highest = [jnp.where(me == n - 1, 1.0, 0.0) for me, n in zip(at, sizes)]

    def iteration(turn, carry):
        pack(PRESSURE, [press_item])
        start(PRESSURE, NY, NX)
        zpairs = jnp.where(upper[1], lroll(zr[VELOCITY, 0], 1), lroll(zr[VELOCITY, 1], -1))
        for x in range(NX):
            k = coefs(kf, x)
            diagonal = aux[2, flat(x)]
            for c in range(3):
                total, here = gather(VELOCITY, vel_item, c, x, k, zpairs)
                res[flat(c * NX + x)] = src[flat(c * NX + x)] - diagonal * here + total
        finish(PRESSURE, NY, NX)
        ar_finish(2, turn - 1)
        add_mean()
        m8 = mean[1]
        m = jnp.concatenate([m8, m8], axis=0)
        zpairs = unpack(PRESSURE, press_item, lowest[1] * m8, highest[1] * m8)
        zfill = jnp.where(low[1], lowest[2], highest[2]) * m
        for x in range(NX):
            inverse = aux[3, flat(x)]
            here, xm, xp, ym, yp = sides(PRESSURE, press_item, 0, x)
            if x == 0:
                xm = xm + lowest[0] * m
            if x == NX - 1:
                xp = xp + highest[0] * m
            zm, zp = ends(here, edge(press_item, 0, x, zpairs) + zfill, 1)
            for c, (a, b) in enumerate(((xm, xp), (ym, yp), (zm, zp))):
                r = res[flat(c * NX + x)] - 0.5 * (b - a)
                res[flat(c * NX + x)] = r
                put(fine, c * NX + x, inverse * r)

        def during(stage):
            if stage == 0:
                acc = jnp.zeros((NY, NZ), jnp.float32)
                for p in range(3 * NX):
                    acc = acc + adj[flat(p)] * res[flat(p)]
                put_sum(acc)
                ar_start(0, turn)
            elif stage == 1:
                ar_finish(0, turn)
                ar_start(1, turn)

        cycle(3, during, False)

        def last_stage():
            ar_finish(1, turn)
            ar_start(2, turn)

        divergence(last_stage, False)
        return carry

    lax.fori_loop(1, SCHUR_ITERS, iteration, 0)

    ar_finish(2, SCHUR_ITERS - 1)
    add_mean()
    m8 = mean[1]
    m = jnp.concatenate([m8, m8], axis=0)
    for x in range(NX):
        out_p[x] = get(press, x) - m
        for c in range(3):
            out_v[c, x] = get(vel, c * NX + x)
        out_t[x] = out_t[x] + RAYLEIGH * get(vel, 2 * NX + x)


def solution(mesh):
    sizes = tuple(mesh.shape[a] for a in AXES)

    def shards(heat, motion, dual, rheology, stiffness):
        cells = heat.size * sizes[0] * sizes[1] * sizes[2]
        vmem = pl.BlockSpec(memory_space=pltpu.VMEM)
        f32 = jnp.float32
        padded = lambda planes: pltpu.VMEM((FIRST + planes * PITCH, NZ), f32)
        flat = lambda planes: pltpu.VMEM((planes * NY, NZ), f32)
        slots = sum(n - 1 for n in sizes)
        return pl.pallas_call(
            functools.partial(kernel, sizes, cells),
            out_shape=(
                jax.ShapeDtypeStruct(heat.shape, f32),
                jax.ShapeDtypeStruct(motion.shape, f32),
                jax.ShapeDtypeStruct(heat.shape, f32),
            ),
            in_specs=[vmem] * 4 + [pl.BlockSpec(memory_space=pltpu.SMEM)],
            out_specs=(vmem,) * 3,
            scratch_shapes=[
                padded(6 * NX), padded(3 * NX), padded(NX), padded(2 * NX),
                flat(6 * NX), flat(3 * NX), flat(3 * NX), flat(3 * NX), padded(2 * NX),
                pltpu.VMEM((7, NX * NY, NZ), f32), pltpu.VMEM((6, EX * ER, NZ), f32), pltpu.VMEM((7, NX * NY, NZ), f32),
                pltpu.VMEM((5, NX * NY, NZ), f32),
                pltpu.VMEM((ROUNDS, 2, 6 * NY, NZ), f32), pltpu.VMEM((ROUNDS, 2, 6 * NY, NZ), f32),
                pltpu.VMEM((ROUNDS, 2, 6 * NX, NZ), f32), pltpu.VMEM((ROUNDS, 2, 6 * NX, NZ), f32),
                pltpu.VMEM((ROUNDS, NY, NZ), f32), pltpu.VMEM((ROUNDS, 2, NY, NZ), f32),
                pltpu.VMEM((8, NZ), f32), pltpu.VMEM((2, 8, NZ), f32),
                pltpu.VMEM((SCHUR_ITERS, 3, 8, NZ), f32), pltpu.VMEM((SCHUR_ITERS, slots, 8, NZ), f32),
                pltpu.VMEM((6 * CX * CY, NZ), f32), pltpu.VMEM((2 * FIRST + 6 * EX * ER, NZ), f32),
                pltpu.VMEM((2 * FIRST + 6 * EX * ER, NZ), f32), pltpu.VMEM((6 * CX * NY, NZ), f32),
                pltpu.VMEM((6 * 6 * 2 * ER, NZ), f32), pltpu.VMEM((6 * CX * 2 * ER, NZ), f32),
                pltpu.VMEM((CX * CY, NZ), f32),
                pltpu.VMEM((2, 2, 9 * CY, NZ), f32), pltpu.VMEM((2, 2, 48, NZ), f32),
                pltpu.VMEM((2, 16, NZ), f32), pltpu.VMEM((2, 2, 8, NZ), f32),
                pltpu.VMEM((2, 2, 9 * CY, NZ), f32), pltpu.VMEM((2, 2, 48, NZ), f32),
                pltpu.VMEM((2, 2, 2, 24, NZ), f32), pltpu.VMEM((2, 3, 2, 16, NZ), f32),
                pltpu.VMEM((2, 3, 2, 2, 8, NZ), f32), pltpu.VMEM((3 * 2 * ER, NZ), f32),
                pltpu.SemaphoreType.DMA((ROUNDS, 6)), pltpu.SemaphoreType.DMA((ROUNDS, 6)),
                pltpu.SemaphoreType.DMA((SCHUR_ITERS, slots)), pltpu.SemaphoreType.DMA((SCHUR_ITERS, slots)),
                pltpu.SemaphoreType.DMA((2, 26)), pltpu.SemaphoreType.DMA((2, 26)),
            ],
            compiler_params=pltpu.CompilerParams(collective_id=0, has_side_effects=True),
        )(heat, motion, dual, rheology, stiffness)

    return jax.shard_map(
        shards,
        mesh=mesh,
        in_specs=(P(*AXES), P(None, *AXES), P(*AXES), P(*AXES), P()),
        out_specs=(P(*AXES), P(None, *AXES), P(*AXES)),
        check_vma=False,
    )
```

```python
import functools

import jax
import jax.numpy as jnp
from jax import lax
from jax.experimental import pallas as pl
from jax.experimental.pallas import tpu as pltpu
from jax.sharding import PartitionSpec as P

RECOMPUTE = 2
SCHUR_ITERS = 4
COARSE_SWEEPS = 3
LAYERS = 8
INCREMENT_DT = 0.2
DIFFUSIVITY = 0.3
ACTIVATION_ENERGY = 2.3
JACOBI_WEIGHT = 0.7
SCHUR_WEIGHT = 0.5
RAYLEIGH = 1.0

MESH = pl.DeviceIdType.MESH
AXES = ("gx", "gy", "gz")
NX, NY, NZ = 8, 16, 128
CX = NX // 2
PITCH = 24
FIRST = 8
KEEP = 1.0 - JACOBI_WEIGHT

HEAT1, HEAT2, FIELDS, PRESSURE, FIRST_SMOOTH, VELOCITY = range(6)
ROUNDS = 6

CY, CZ = NY // 2, NZ // 2
DEPTH = COARSE_SWEEPS
EX = CX + 2 * DEPTH
ER = 16
COARSE_VISC, COARSE_ITERATE = range(2)
AROUND = [(dx, dy, dz) for dx in (-1, 1, 0) for dz in (-1, 1, 0) for dy in (-1, 1, 0) if (dx, dy, dz) != (0, 0, 0)]
ENDS_FIRST = (0, NX - 1) + tuple(range(1, NX - 1))


def row(plane):
    return FIRST + plane * PITCH


class Item:
    def __init__(self, ref, comps, planes, width, xoff=0, yoff=0, lane=0, first=0):
        self.ref, self.comps, self.planes, self.width = ref, comps, planes, width
        self.xoff, self.yoff, self.lane, self.first = xoff, yoff, lane, first

    def count(self):
        return self.comps * self.planes

    def spot(self, c, x):
        return self.lane + (c * self.planes + x) * 2 * self.width


def kernel(sizes, total_cells, heat, motion, dual, rheology, stiffness, out_t, out_v, out_p, out_m, fine, vel, press,
           fields, res, src, adj, held, sums, trans, kf, kc, kh, aux, xs, xr, ys, yr, zs, zr, psum, mean, ar_out, ar_in,
           own, wide, swept, halves, grown, grown_ends, cinv, cxs, cys, czs, czys, cxr, cyr, cxyr, czr, czyr, zq,
           send_sem, recv_sem, ar_send, ar_recv, c_send, c_recv):
    at = [lax.axis_index(a) for a in AXES]
    barrier = pltpu.get_barrier_semaphore()
    after = [lax.rem(me + 1, n) for me, n in zip(at, sizes)]
    before = [lax.rem(me + n - 1, n) for me, n in zip(at, sizes)]
    up, down = [me < n - 1 for me, n in zip(at, sizes)], [me > 0 for me in at]

    def there(d):
        ok = None
        for k, step in enumerate(d):
            if step:
                inside = up[k] if step > 0 else down[k]
                ok = inside if ok is None else jnp.logical_and(ok, inside)
        return ok

    exists = {d: there(d) for d in AROUND}
    beside = {d: {axis: after[k] if d[k] > 0 else before[k] for k, axis in enumerate(AXES) if d[k]} for d in AROUND}
    line = []
    for axis, me, n in zip(AXES, at, sizes):
        line.append([{axis: lax.rem(me + d, n)} for d in range(1, n)])
    peers = sum(n - 1 for n in sizes)
    for others in line:
        for other in others:
            pl.semaphore_signal(barrier, inc=1, device_id=other, device_id_type=MESH)
    for d in AROUND:
        if sum(map(abs, d)) > 1:
            @pl.when(exists[d])
            def _():
                pl.semaphore_signal(barrier, inc=1, device_id=beside[d], device_id_type=MESH)
            peers = peers + exists[d].astype(jnp.int32)

    lanes = lax.broadcasted_iota(jnp.int32, (NY, NZ), 1)
    rows = lax.broadcasted_iota(jnp.int32, (NY, NZ), 0)
    pair = {1: lanes >> 1, 2: lanes >> 2}
    upper = {1: (lanes & 1) == 1, 2: (lanes & 3) >= 2}
    low = {1: lanes < 1, 2: lanes < 2}
    high = {1: lanes >= NZ - 1, 2: lanes >= NZ - 2}
    even_row = (rows & 1) == 0
    even_lane = (lanes & 1) == 0

    def lroll(v, shift):
        return pltpu.roll(v, shift % NZ, 1)

    def copies(t, xrows, yrows, axes):
        out = []
        for k in axes:
            for s in (0, 1):
                source = (xs.at[t, s, pl.ds(0, xrows)], ys.at[t, s, pl.ds(0, yrows)], zs.at[t])[k]
                target = (xr.at[t, s, pl.ds(0, xrows)], yr.at[t, s, pl.ds(0, yrows)], zr.at[t, s])[k]
                step = 1 if s == 0 else -1
                d = tuple(step if axis == k else 0 for axis in range(3))
                opposite = tuple(-v for v in d)
                copy = pltpu.make_async_remote_copy(
                    src_ref=source, dst_ref=target, send_sem=send_sem.at[t, 2 * k + s],
                    recv_sem=recv_sem.at[t, 2 * k + s], device_id=beside[d], device_id_type=MESH)
                out.append((copy, exists[d], exists[opposite]))
        return out

    def start(t, xrows, yrows, axes):
        for copy, sends, _ in copies(t, xrows, yrows, axes):
            pl.when(sends)(copy.start)

    def finish(t, xrows, yrows):
        for copy, _, gets in copies(t, xrows, yrows, (1, 2, 0)):
            pl.when(gets)(copy.wait_recv)
        for copy, sends, _ in copies(t, xrows, yrows, (1, 2, 0)):
            pl.when(sends)(copy.wait_send)

    def pack_lanes(acc, value, spot, w):
        return jnp.where(pair[w] == spot // (2 * w), lroll(value, spot + w), acc)

    def chunks(n):
        return [(a, min(8, n - a)) for a in range(0, n, 8)]

    def extent(items):
        return sum(it.comps for it in items) * NY, sum(it.count() for it in items)

    def send_x(t, items):
        for it in items:
            for c in range(it.comps):
                p = (it.first + c) * it.planes
                at_row = it.xoff + c * NY
                xs[t, 0, at_row:at_row + NY] = it.ref[row(p + it.planes - 1):row(p + it.planes - 1) + NY]
                xs[t, 1, at_row:at_row + NY] = it.ref[row(p):row(p) + NY]
        start(t, *extent(items), (0,))

    def send_yz(t, items):
        acc = jnp.zeros((NY, NZ), jnp.float32)
        for it in items:
            for c in range(it.comps):
                for x in range(it.planes):
                    r = row((it.first + c) * it.planes + x)
                    acc = pack_lanes(acc, it.ref[r:r + NY], it.spot(c, x), it.width)
        zs[t] = acc
        start(t, *extent(items), (2,))
        for it in items:
            base = row(it.first * it.planes)
            for a, size in chunks(it.count()):
                ys[t, 0, it.yoff + a:it.yoff + a + size] = it.ref[pl.ds(base + a * PITCH + NY - 1, size, stride=PITCH), :]
                ys[t, 1, it.yoff + a:it.yoff + a + size] = it.ref[pl.ds(base + a * PITCH, size, stride=PITCH), :]
        start(t, *extent(items), (1,))

    def unpack(t, it, low_extra=None, high_extra=None):
        base = row(it.first * it.planes)
        for a, size in chunks(it.count()):
            below, above = yr[t, 0, it.yoff + a:it.yoff + a + size], yr[t, 1, it.yoff + a:it.yoff + a + size]
            if low_extra is not None:
                below, above = below + low_extra[:size], above + high_extra[:size]
            for k in range(it.width):
                it.ref[pl.ds(base + a * PITCH - 1 - k, size, stride=PITCH), :] = below
                it.ref[pl.ds(base + a * PITCH + NY + k, size, stride=PITCH), :] = above
        return jnp.where(upper[it.width], lroll(zr[t, 0], it.width), lroll(zr[t, 1], -it.width))

    def sides(t, it, c, x):
        r, k = row((it.first + c) * it.planes + x), it.xoff + c * NY
        here = it.ref[r:r + NY]
        xm = xr[t, 0, k:k + NY] if x == 0 else it.ref[r - PITCH:r - PITCH + NY]
        xp = xr[t, 1, k:k + NY] if x == it.planes - 1 else it.ref[r + PITCH:r + PITCH + NY]
        w = it.width
        return here, xm, xp, it.ref[r - w:r - w + NY], it.ref[r + w:r + w + NY]

    def edge(it, c, x, zpairs):
        return lroll(zpairs, -(it.spot(c, x) + it.width))

    def ends(here, at_edge, w):
        return jnp.where(low[w], at_edge, lroll(here, w)), jnp.where(high[w], at_edge, lroll(here, -w))

    def coefs(k, x):
        return [k[n, x * NY:(x + 1) * NY] for n in range(7)]

    def set_coefs(k, x, six, w):
        xm, xp, ym, yp, zm, zp = six
        for n, v in enumerate((xm, xp, ym, yp, jnp.where(low[w], 0.0, zm), jnp.where(high[w], 0.0, zp),
                               jnp.where(low[w], zm, jnp.where(high[w], zp, 0.0)))):
            k[n, x * NY:(x + 1) * NY] = v

    def gather(t, it, c, x, k, zpairs):
        here, xm, xp, ym, yp = sides(t, it, c, x)
        w = it.width
        total = (k[0] * xm + k[1] * xp) + (k[2] * ym + k[3] * yp)
        total = total + (k[4] * lroll(here, w) + k[5] * lroll(here, -w)) + k[6] * edge(it, c, x, zpairs)
        return total, here

    def put(ref, plane, value):
        ref[row(plane):row(plane) + NY] = value

    def get(ref, plane):
        return ref[row(plane):row(plane) + NY]

    def flat(plane):
        return slice(plane * NY, (plane + 1) * NY)

    lanes8 = lax.broadcasted_iota(jnp.int32, (CY, NZ), 1)
    left8 = lanes8 < CZ
    left = lanes < CZ
    left4 = lax.broadcasted_iota(jnp.int32, (4, NZ), 1) < CZ
    squeeze = 2 * (lanes8 & (CZ - 1))
    repeat = lanes >> 1
    outer = jnp.where(lanes == 0, NZ - 1, CZ)
    beyond = jnp.where(lanes >= NZ - DEPTH, lanes - (NZ - DEPTH), (lanes - CZ + DEPTH) & 7)

    def take(v, index):
        return jnp.take_along_axis(v, index, axis=1)

    def tile(p):
        return slice(p * CY, (p + 1) * CY)

    def restrict(slot, a, b):
        r = slot * NY
        halves[r:r + NY] = a + b
        t = halves[pl.ds(r, CY, stride=2), :] + halves[pl.ds(r + 1, CY, stride=2), :]
        return take(t + lroll(t, -1), squeeze) * 0.125

    def c_copies(t, nc):
        xr_n, yr_n, z_n = (3 * nc + 1) // 2 * CY, 8 * nc, (CX * nc + 15) // 16 * CY
        out = []
        for i, d in enumerate(AROUND):
            dx, dy, dz = d
            hx, hy, hz = (dx < 0) * 1, (dy < 0) * 1, (dz < 0) * 1
            if dz:
                if dy:
                    source = czys.at[t, hy, pl.ds(0, z_n // 2)]
                    target = czyr.at[t, dx + 1, hy, hz, pl.ds(0, z_n // 2)]
                else:
                    source, target = czs.at[t, pl.ds(0, z_n)], czr.at[t, dx + 1, hz, pl.ds(0, z_n)]
            elif dx and dy:
                source = cys.at[t, hy, pl.ds(0 if dx < 0 else 4 * nc, 4 * nc)]
                target = cxyr.at[t, hx, hy, pl.ds(0, 4 * nc)]
            elif dy:
                source, target = cys.at[t, hy, pl.ds(0, yr_n)], cyr.at[t, hy, pl.ds(0, yr_n)]
            else:
                source, target = cxs.at[t, hx, pl.ds(0, xr_n)], cxr.at[t, hx, pl.ds(0, xr_n)]
            copy = pltpu.make_async_remote_copy(
                src_ref=source, dst_ref=target, send_sem=c_send.at[t, i], recv_sem=c_recv.at[t, i],
                device_id=beside[d], device_id_type=MESH)
            out.append((copy, exists[d], exists[tuple(-v for v in d)]))
        return out

    def c_start(t, nc):
        for part in range((CX * nc + 15) // 16):
            acc = jnp.zeros((CY, NZ), jnp.float32)
            for g in range(16 * part, min(16 * part + 16, CX * nc)):
                spot = g % 16 * 8
                acc = jnp.where((lanes8 >> 3) == g % 16, lroll(own[tile(g)], spot - (CZ - DEPTH)), acc)
            czs[t, tile(part)] = acc
            czys[t, 0, 4 * part:4 * part + 4] = acc[4:8]
            czys[t, 1, 4 * part:4 * part + 4] = acc[0:4]
        copies26 = c_copies(t, nc)
        def go(kind):
            for d, (copy, sends, _) in zip(AROUND, copies26):
                if kind(d):
                    pl.when(sends)(copy.start)
        go(lambda d: d[0] and d[2])
        for h, first in ((0, 1), (1, 0)):
            for q in range((3 * nc + 1) // 2):
                a, b = first * nc + 2 * q, first * nc + min(2 * q + 1, 3 * nc - 1)
                cxs[t, h, tile(q)] = jnp.where(left8, own[tile(a)], own[tile(b)])
        go(lambda d: d == (1, 0, 0) or d == (-1, 0, 0))
        for h, rows_from in ((0, 4), (1, 0)):
            for q in range(2 * nc):
                a, b = 2 * q * CY + rows_from, (2 * q + 1) * CY + rows_from
                cys[t, h, 4 * q:4 * q + 4] = jnp.where(left4, own[a:a + 4], own[b:b + 4])
        go(lambda d: d[0] and d[1] and not d[2])
        go(lambda d: not d[0])

    def c_finish(t, nc):
        for copy, _, gets in c_copies(t, nc):
            pl.when(gets)(copy.wait_recv)
        for copy, sends, _ in c_copies(t, nc):
            pl.when(sends)(copy.wait_send)

    def wide_row(c, e):
        return FIRST + (c * EX + e) * ER

    def assemble(t, nc):
        group = (lanes8 & 7) < DEPTH
        group4 = (lax.broadcasted_iota(jnp.int32, (4, NZ), 1) & 7) < DEPTH
        for dx in range(3):
            for part in range((CX * nc + 15) // 16):
                r = (dx * 2 + part) * ER
                zq[r + 4:r + 12] = jnp.where(group, czr[t, dx, 0, tile(part)], czr[t, dx, 1, tile(part)])
                for h, at_row in ((0, 0), (1, 12)):
                    four = slice(4 * part, 4 * part + 4)
                    zq[r + at_row:r + at_row + 4] = jnp.where(group4, czyr[t, dx, h, 0, four], czyr[t, dx, h, 1, four])
        for c in range(nc):
            for e in range(EX):
                x = e - DEPTH
                r = wide_row(c, e)
                if 0 <= x < CX:
                    dx, sender = 0, x
                elif x < 0:
                    dx, sender = -1, x + CX
                else:
                    dx, sender = 1, x - CX
                p = sender * nc + c
                if dx == 0:
                    wide[r + 4:r + 12] = own[tile(p)]
                else:
                    i = p - (nc if dx < 0 else 0)
                    v = cxr[t, 0 if dx < 0 else 1, tile(i // 2)]
                    wide[r + 4:r + 12] = v if i % 2 == 0 else lroll(v, CZ)
                if -DEPTH < x < CX + DEPTH - 1:
                    q = p // 2
                    for h, at_row in ((0, 0), (1, 12)):
                        if dx == 0:
                            v = cyr[t, h, 4 * q:4 * q + 4]
                        else:
                            k = 4 * (q - (nc if dx < 0 else 0))
                            v = cxyr[t, 0 if dx < 0 else 1, h, k:k + 4]
                        wide[r + at_row:r + at_row + 4] = v if p % 2 == 0 else lroll(v, CZ)
                    g = p
                    z = zq[((dx_from(dx)) * 2 + g // 16) * ER:((dx_from(dx)) * 2 + g // 16) * ER + ER]
                    wide[r:r + ER] = jnp.where(left, wide[r:r + ER], take(z, (beyond + g % 16 * 8) & (NZ - 1)))

    def dx_from(dx):
        return 1 - dx

    def sweep(source, target, c, e, keep):
        r = wide_row(c, e)
        k = [kc[n, e * ER:(e + 1) * ER] for n in range(6)]
        here = source[r:r + ER]
        total = keep * here + k[0] * source[r - ER:r] + k[1] * source[r + ER:r + 2 * ER]
        total = total + k[2] * source[r - 1:r - 1 + ER] + k[3] * source[r + 1:r + 1 + ER]
        return total + k[4] * lroll(here, 1) + k[5] * lroll(here, -1)

    order = (1, 2, 0)
    base_slot = {}
    slots = 0
    for axis in order:
        base_slot[axis] = slots
        slots += sizes[axis] - 1

    def ar_copies(axis, turn):
        n = sizes[axis]
        out = []
        for d in range(1, n):
            slot = base_slot[axis] + d - 1
            out.append(pltpu.make_async_remote_copy(
                src_ref=ar_out.at[turn, order.index(axis)], dst_ref=ar_in.at[turn, slot],
                send_sem=ar_send.at[turn, slot], recv_sem=ar_recv.at[turn, slot],
                device_id=line[axis][d - 1], device_id_type=MESH))
        return out

    def ar_start(stage, turn):
        ar_out[turn, stage] = psum[...]
        for copy in ar_copies(order[stage], turn):
            copy.start()

    def ar_finish(stage, turn):
        axis = order[stage]
        pending = ar_copies(axis, turn)
        total = psum[...]
        for copy in pending:
            copy.wait_recv()
        for d in range(1, sizes[axis]):
            total = total + ar_in[turn, base_slot[axis] + d - 1]
        psum[...] = total
        for copy in pending:
            copy.wait_send()

    def put_sum(value):
        s = jnp.sum(jnp.sum(value, axis=0, keepdims=True), axis=1, keepdims=True)
        psum[...] = jnp.broadcast_to(s, (8, NZ))

    def add_mean():
        mean[0] = mean[0] + psum[...]
        mean[1] = mean[1] + (0.5 / total_cells) * mean[0]

    for k, (me, n) in enumerate(zip(at, sizes)):
        for s, gone in ((0, me == 0), (1, me == n - 1)):
            @pl.when(gone)
            def _():
                for t in range(ROUNDS):
                    into = (xr, yr, zr)[k]
                    into[t, s] = jnp.zeros(into.shape[2:], jnp.float32)

    for d in AROUND:
        @pl.when(jnp.logical_not(exists[tuple(-v for v in d)]))
        def _():
            dx, dy, dz = d
            hx, hy, hz = (dx < 0) * 1, (dy < 0) * 1, (dz < 0) * 1
            for t in range(2):
                if dz and dy:
                    into = czyr.at[t, dx + 1, hy, hz]
                elif dz:
                    into = czr.at[t, dx + 1, hz]
                elif dx and dy:
                    into = cxyr.at[t, hx, hy]
                elif dy:
                    into = cyr.at[t, hy]
                else:
                    into = cxr.at[t, hx]
                into[...] = jnp.zeros(into.shape, jnp.float32)

    wide[...] = jnp.zeros_like(wide)
    mean[...] = jnp.zeros_like(mean)
    heat_item = Item(fields, 1, NX, 1)
    trans_item = Item(trans, 1, NX, 1, xoff=NY, yoff=NX, lane=2 * NX)
    spread, step = INCREMENT_DT * DIFFUSIVITY, INCREMENT_DT
    for x in range(NX):
        put(fields, x, heat[x])
        lam = dual[x]
        six, total = [], 0.0
        for k in range(3):
            m = motion[k, x]
            am, ap = spread + step * jnp.maximum(m, 0.0), spread - step * jnp.minimum(m, 0.0)
            six += [am, ap]
            total = total + am + ap
        set_coefs(kh, x, six, 1)
        aux[0, flat(x)] = 1.0 - total
        if x == 0:
            xs[HEAT1, 1, NY:2 * NY] = six[0] * lam
        if x == NX - 1:
            xs[HEAT1, 0, NY:2 * NY] = six[1] * lam
        put(trans, x, six[3] * lam)
        put(trans, NX + x, six[2] * lam)
    acc = jnp.zeros((NY, NZ), jnp.float32)
    xs[HEAT1, 0, 0:NY] = heat[NX - 1]
    xs[HEAT1, 1, 0:NY] = heat[0]
    ys[HEAT1, 0, 0:NX] = fields[pl.ds(FIRST + NY - 1, NX, stride=PITCH), :]
    ys[HEAT1, 1, 0:NX] = fields[pl.ds(FIRST, NX, stride=PITCH), :]
    ys[HEAT1, 0, NX:2 * NX] = trans[pl.ds(FIRST + NY - 1, NX, stride=PITCH), :]
    ys[HEAT1, 1, NX:2 * NX] = trans[pl.ds(row(NX), NX, stride=PITCH), :]
    for x in range(NX):
        lam = dual[x]
        acc = pack_lanes(acc, heat[x], heat_item.spot(0, x), 1)
        am = spread + step * jnp.maximum(motion[2, x], 0.0)
        ap = spread - step * jnp.minimum(motion[2, x], 0.0)
        acc = pack_lanes(acc, jnp.where(low[1], am * lam, ap * lam), trans_item.spot(0, x), 1)
    zs[HEAT1] = acc
    pl.semaphore_wait(barrier, peers)
    start(HEAT1, 2 * NY, 2 * NX, (0, 2, 1))
    for x in range(NX):
        base = jnp.zeros((NY, NZ), jnp.float32)
        for layer in range(LAYERS):
            base = jnp.where(rheology[x] == layer, stiffness[layer], base)
        aux[1, flat(x)] = base
    finish(HEAT1, 2 * NY, 2 * NX)

    zpairs = unpack(HEAT1, heat_item)
    next_item = Item(fields, 1, NX, 1, first=2)
    for x in ENDS_FIRST:
        total, here = gather(HEAT1, heat_item, 0, x, coefs(kh, x), zpairs)
        put(fields, 2 * NX + x, aux[0, flat(x)] * here + total)
        if x == NX - 1:
            send_x(HEAT2, [next_item])
    send_yz(HEAT2, [next_item])

    trans[pl.ds(row(0) - 1, NX, stride=PITCH), :] = yr[HEAT1, 0, NX:2 * NX]
    trans[pl.ds(row(NX) + NY, NX, stride=PITCH), :] = yr[HEAT1, 1, NX:2 * NX]
    for x in range(NX):
        lam = dual[x]
        ap_x = lambda i: (spread - step * jnp.minimum(motion[0, i], 0.0)) * dual[i]
        am_x = lambda i: (spread + step * jnp.maximum(motion[0, i], 0.0)) * dual[i]
        below = xr[HEAT1, 0, NY:2 * NY] if x == 0 else ap_x(x - 1)
        above = xr[HEAT1, 1, NY:2 * NY] if x == NX - 1 else am_x(x + 1)
        r = row(x)
        total = aux[0, flat(x)] * lam + below + above
        total = total + trans[r - 1:r - 1 + NY] + trans[row(NX + x) + 1:row(NX + x) + 1 + NY]
        am = spread + step * jnp.maximum(motion[2, x], 0.0)
        ap = spread - step * jnp.minimum(motion[2, x], 0.0)
        at_edge = edge(trans_item, 0, x, zpairs)
        total = total + jnp.where(low[1], at_edge, lroll(ap * lam, 1)) + jnp.where(high[1], at_edge, lroll(am * lam, -1))
        out_t[x] = total
    finish(HEAT2, NY, NX)

    zpairs = unpack(HEAT2, next_item)
    both = Item(fields, 2, NX, 1)
    for x in ENDS_FIRST:
        total, here = gather(HEAT2, next_item, 0, x, coefs(kh, x), zpairs)
        t2 = aux[0, flat(x)] * here + total
        put(fields, x, t2)
        put(fields, NX + x, aux[1, flat(x)] * jnp.exp(-ACTIVATION_ENERGY * t2))
        if x == NX - 1:
            send_x(FIELDS, [both])
    for x in range(CX):
        own[tile(x)] = restrict(x, get(fields, NX + 2 * x), get(fields, NX + 2 * x + 1))
    c_start(COARSE_VISC, 1)
    send_yz(FIELDS, [both])
    finish(FIELDS, 2 * NY, 2 * NX)

    zpairs = unpack(FIELDS, both)
    six_item = Item(fine, 6, NX, 1)
    for x in ENDS_FIRST:
        here, xm, xp, ym, yp = sides(FIELDS, both, 0, x)
        zm, zp = ends(here, edge(both, 0, x, zpairs), 1)
        lam = -INCREMENT_DT * dual[x]
        for k, (m, p) in enumerate(((xm, xp), (ym, yp), (zm, zp))):
            src[flat(k * NX + x)] = lam * jnp.where(motion[k, x] > 0, here - m, p - here)
        here, xm, xp, ym, yp = sides(FIELDS, both, 1, x)
        zm, zp = ends(here, edge(both, 1, x, zpairs), 1)
        six = [0.5 * (here + v) for v in (xm, xp, ym, yp, zm, zp)]
        set_coefs(kf, x, six, 1)
        diagonal = (six[0] + six[1]) + (six[2] + six[3]) + (six[4] + six[5])
        inverse = JACOBI_WEIGHT / diagonal
        aux[2, flat(x)] = diagonal
        aux[3, flat(x)] = inverse
        aux[4, flat(x)] = (0.5 * SCHUR_WEIGHT) * here
        for k, (m, p) in enumerate(((xm, xp), (ym, yp), (zm, zp))):
            g = 0.5 * (p - m)
            s = src[flat(k * NX + x)]
            res[flat((3 + k) * NX + x)] = g
            res[flat(k * NX + x)] = s
            put(fine, (3 + k) * NX + x, inverse * g)
            put(fine, k * NX + x, inverse * s)
        if x == NX - 1:
            send_x(FIRST_SMOOTH, [six_item])
    send_yz(FIRST_SMOOTH, [six_item])
    c_finish(COARSE_VISC, 1)
    assemble(COARSE_VISC, 1)
    inside_rows = jnp.logical_and(jnp.logical_or(rows >= 4, at[1] > 0), jnp.logical_or(rows < 12, at[1] < sizes[1] - 1))
    inside = jnp.logical_or(left, jnp.logical_or(
        jnp.logical_and(lanes >= NZ - DEPTH, at[2] > 0),
        jnp.logical_and(lanes < CZ + DEPTH, at[2] < sizes[2] - 1)))
    inside = jnp.logical_and(inside, inside_rows)
    for e in range(1, EX - 1):
        r = wide_row(0, e)
        here = wide[r:r + ER]
        others = (wide[r - ER:r], wide[r + ER:r + 2 * ER], wide[r - 1:r - 1 + ER], wide[r + 1:r + 1 + ER],
                  lroll(here, 1), lroll(here, -1))
        six = [0.125 * (here + v) for v in others]
        ok = inside
        if e < DEPTH:
            ok = jnp.logical_and(ok, at[0] > 0)
        elif e >= DEPTH + CX:
            ok = jnp.logical_and(ok, at[0] < sizes[0] - 1)
        inverse = jnp.where(ok, JACOBI_WEIGHT / ((six[0] + six[1]) + (six[2] + six[3]) + (six[4] + six[5])), 0.0)
        for n in range(6):
            kc[n, e * ER:(e + 1) * ER] = jnp.where(ok, inverse * six[n], 0.0)
        if DEPTH <= e < DEPTH + CX:
            grown[0:ER] = inverse
            cinv[tile(e - DEPTH)] = take(grown[4:12], lanes8 & (CZ - 1))

    vel_item, press_item = Item(vel, 3, NX, 1), Item(press, 1, NX, 1)

    def cycle(nc, during, first):
        fi = Item(fine, nc, NX, 1)
        fx, fy = nc * NY, nc * NX
        during(0)
        finish(FIRST_SMOOTH, fx, fy)
        zpairs = unpack(FIRST_SMOOTH, fi)
        for x in range(CX):
            ka, kb = coefs(kf, 2 * x), coefs(kf, 2 * x + 1)
            for c in range(nc):
                pa, pb = c * NX + 2 * x, c * NX + 2 * x + 1
                a = gather(FIRST_SMOOTH, fi, c, 2 * x, ka, zpairs)[0]
                b = gather(FIRST_SMOOTH, fi, c, 2 * x + 1, kb, zpairs)[0]
                sums[flat(pa)] = a
                sums[flat(pb)] = b
                a = KEEP * res[flat(pa)] + a
                b = KEEP * res[flat(pb)] + b
                if first and c >= 3:
                    held[flat(pa - 3 * NX)] = a
                    held[flat(pb - 3 * NX)] = b
                own[tile(x * nc + c)] = cinv[tile(x)] * restrict(x * nc + c, a, b)
        c_start(COARSE_ITERATE, nc)
        during(1)
        acc = jnp.zeros((NY, NZ), jnp.float32)
        for x in range(NX):
            inverse = aux[3, flat(x)]
            for c in range(nc):
                p = c * NX + x
                here = get(fine, p)
                part = (1.0 + KEEP) * here + inverse * sums[flat(p)]
                if c >= 3:
                    adj[flat(p - 3 * NX)] = part
                elif first:
                    put(vel, p, part)
                    acc = acc + held[flat(p)] * here + get(fine, 3 * NX + p) * res[flat(p)]
                else:
                    put(vel, p, get(vel, p) + part)
        c_finish(COARSE_ITERATE, nc)
        assemble(COARSE_ITERATE, nc)
        for e in range(1, EX - 1):
            for c in range(nc):
                r = wide_row(c, e)
                swept[r:r + ER] = sweep(wide, swept, c, e, 2.0 - JACOBI_WEIGHT)
        for e in range(2, EX - 2):
            for c in range(nc):
                r = wide_row(c, e)
                v = wide[r:r + ER] + sweep(swept, None, c, e, KEEP)
                base = (c * 6 + e - 2) * 2 * ER
                full = take(v, repeat)
                for k in (0, 8):
                    for odd in (0, 1):
                        grown[pl.ds(base + 2 * k + odd, 8, stride=2), :] = full[k:k + 8]
                if DEPTH <= e < DEPTH + CX:
                    base = (c * CX + e - DEPTH) * 2 * ER
                    full = take(v, outer)
                    for k in (0, 8):
                        for odd in (0, 1):
                            grown_ends[pl.ds(base + 2 * k + odd, 8, stride=2), :] = full[k:k + 8]

        if first:
            for x in range(NX):
                for c in range(3):
                    base = (c * 6 + x // 2 + 1) * 2 * ER + FIRST
                    acc = acc + held[flat(c * NX + x)] * grown[base:base + NY]
            put_sum(acc)
            ar_start(0, 0)
        for x in ENDS_FIRST:
            k = coefs(kf, x)
            inverse = aux[3, flat(x)]
            for c in range(nc):
                base = [(c * 6 + q // 2 + 1) * 2 * ER + FIRST for q in (x - 1, x, x + 1)]
                here = grown[base[1]:base[1] + NY]
                total = k[0] * grown[base[0]:base[0] + NY] + k[1] * grown[base[2]:base[2] + NY]
                total = total + k[2] * grown[base[1] - 1:base[1] - 1 + NY] + k[3] * grown[base[1] + 1:base[1] + 1 + NY]
                at_edge = (c * CX + x // 2) * 2 * ER + FIRST
                total = total + (k[4] * lroll(here, 1) + k[5] * lroll(here, -1)) + k[6] * grown_ends[at_edge:at_edge + NY]
                part = KEEP * here + inverse * total
                p = c * NX + x
                if c >= 3:
                    adj[flat(p - 3 * NX)] = adj[flat(p - 3 * NX)] + part
                else:
                    put(vel, p, get(vel, p) + part)
            if x == NX - 1:
                send_x(VELOCITY, [vel_item])
        send_yz(VELOCITY, [vel_item])

    def divergence(during, first, send):
        during()
        finish(VELOCITY, 3 * NY, 3 * NX)
        zpairs = unpack(VELOCITY, vel_item)
        for x in ENDS_FIRST:
            _, xm, xp, _, _ = sides(VELOCITY, vel_item, 0, x)
            _, _, _, ym, yp = sides(VELOCITY, vel_item, 1, x)
            here = get(vel, 2 * NX + x)
            zm, zp = ends(here, edge(vel_item, 2, x, zpairs), 1)
            change = aux[4, flat(x)] * ((xp - xm) + (yp - ym) + (zp - zm))
            put(press, x, -change if first else get(press, x) - change)
            if x == NX - 1 and send is not None:
                send()

    cycle(6, lambda stage: None, True)

    def first_sum():
        ar_finish(0, 0)
        ar_start(1, 0)

    def send_pressure():
        send_x(PRESSURE, [press_item])

    divergence(first_sum, True, send_pressure)
    send_yz(PRESSURE, [press_item])
    ar_finish(1, 0)
    ar_start(2, 0)

    lowest = [jnp.where(me == 0, 1.0, 0.0) for me in at]
    highest = [jnp.where(me == n - 1, 1.0, 0.0) for me, n in zip(at, sizes)]

    def iteration(turn, carry):
        zpairs = jnp.where(upper[1], lroll(zr[VELOCITY, 0], 1), lroll(zr[VELOCITY, 1], -1))
        for x in range(NX):
            k = coefs(kf, x)
            diagonal = aux[2, flat(x)]
            for c in range(3):
                total, here = gather(VELOCITY, vel_item, c, x, k, zpairs)
                res[flat(c * NX + x)] = src[flat(c * NX + x)] - diagonal * here + total
        finish(PRESSURE, NY, NX)
        ar_finish(2, turn - 1)
        add_mean()
        m8 = mean[1]
        m = jnp.concatenate([m8, m8], axis=0)
        zpairs = unpack(PRESSURE, press_item, lowest[1] * m8, highest[1] * m8)
        zfill = jnp.where(low[1], lowest[2], highest[2]) * m
        three = Item(fine, 3, NX, 1)
        for x in ENDS_FIRST:
            inverse = aux[3, flat(x)]
            here, xm, xp, ym, yp = sides(PRESSURE, press_item, 0, x)
            if x == 0:
                xm = xm + lowest[0] * m
            if x == NX - 1:
                xp = xp + highest[0] * m
            zm, zp = ends(here, edge(press_item, 0, x, zpairs) + zfill, 1)
            for c, (a, b) in enumerate(((xm, xp), (ym, yp), (zm, zp))):
                r = res[flat(c * NX + x)] - 0.5 * (b - a)
                res[flat(c * NX + x)] = r
                put(fine, c * NX + x, inverse * r)
            if x == NX - 1:
                send_x(FIRST_SMOOTH, [three])
        send_yz(FIRST_SMOOTH, [three])

        def during(stage):
            if stage == 0:
                acc = jnp.zeros((NY, NZ), jnp.float32)
                for p in range(3 * NX):
                    acc = acc + adj[flat(p)] * res[flat(p)]
                put_sum(acc)
                ar_start(0, turn)
            elif stage == 1:
                ar_finish(0, turn)
                ar_start(1, turn)

        cycle(3, during, False)

        def last_stage():
            ar_finish(1, turn)
            ar_start(2, turn)

        not_last = turn < SCHUR_ITERS - 1
        divergence(last_stage, False, lambda: pl.when(not_last)(send_pressure))

        @pl.when(not_last)
        def _():
            send_yz(PRESSURE, [press_item])
        return carry

    lax.fori_loop(1, SCHUR_ITERS, iteration, 0)

    ar_finish(2, SCHUR_ITERS - 1)
    add_mean()
    out_m[...] = mean[1]
    for x in range(NX):
        out_p[x] = get(press, x)
        for c in range(3):
            out_v[c, x] = get(vel, c * NX + x)


def outputs(transported, velocity, pressure, mean, out_t, out_v, out_p):
    out_t[...] = transported[...] + RAYLEIGH * velocity[2]
    out_v[...] = velocity[...]
    m = mean[...]
    out_p[...] = pressure[...] - jnp.concatenate([m, m], axis=0)[None]


def solution(mesh):
    sizes = tuple(mesh.shape[a] for a in AXES)

    def shards(heat, motion, dual, rheology, stiffness):
        cells = heat.size * sizes[0] * sizes[1] * sizes[2]
        vmem = pl.BlockSpec(memory_space=pltpu.VMEM)
        f32 = jnp.float32
        padded = lambda planes: pltpu.VMEM((FIRST + planes * PITCH, NZ), f32)
        flat = lambda planes: pltpu.VMEM((planes * NY, NZ), f32)
        slots = sum(n - 1 for n in sizes)
        found = (
            jax.ShapeDtypeStruct(heat.shape, f32),
            jax.ShapeDtypeStruct(motion.shape, f32),
            jax.ShapeDtypeStruct(heat.shape, f32),
        )
        parts = pl.pallas_call(
            functools.partial(kernel, sizes, cells),
            out_shape=found + (jax.ShapeDtypeStruct((8, NZ), f32),),
            in_specs=[vmem] * 4 + [pl.BlockSpec(memory_space=pltpu.SMEM)],
            out_specs=(vmem,) * 4,
            scratch_shapes=[
                padded(6 * NX), padded(3 * NX), padded(NX), padded(3 * NX),
                flat(6 * NX), flat(3 * NX), flat(3 * NX), flat(3 * NX), flat(6 * NX), padded(2 * NX),
                pltpu.VMEM((7, NX * NY, NZ), f32), pltpu.VMEM((6, EX * ER, NZ), f32), pltpu.VMEM((7, NX * NY, NZ), f32),
                pltpu.VMEM((5, NX * NY, NZ), f32),
                pltpu.VMEM((ROUNDS, 2, 6 * NY, NZ), f32), pltpu.VMEM((ROUNDS, 2, 6 * NY, NZ), f32),
                pltpu.VMEM((ROUNDS, 2, 6 * NX, NZ), f32), pltpu.VMEM((ROUNDS, 2, 6 * NX, NZ), f32),
                pltpu.VMEM((ROUNDS, NY, NZ), f32), pltpu.VMEM((ROUNDS, 2, NY, NZ), f32),
                pltpu.VMEM((8, NZ), f32), pltpu.VMEM((2, 8, NZ), f32),
                pltpu.VMEM((SCHUR_ITERS, 3, 8, NZ), f32), pltpu.VMEM((SCHUR_ITERS, slots, 8, NZ), f32),
                pltpu.VMEM((6 * CX * CY, NZ), f32), pltpu.VMEM((2 * FIRST + 6 * EX * ER, NZ), f32),
                pltpu.VMEM((2 * FIRST + 6 * EX * ER, NZ), f32), pltpu.VMEM((6 * CX * NY, NZ), f32),
                pltpu.VMEM((6 * 6 * 2 * ER, NZ), f32), pltpu.VMEM((6 * CX * 2 * ER, NZ), f32),
                pltpu.VMEM((CX * CY, NZ), f32),
                pltpu.VMEM((2, 2, 9 * CY, NZ), f32), pltpu.VMEM((2, 2, 48, NZ), f32),
                pltpu.VMEM((2, 16, NZ), f32), pltpu.VMEM((2, 2, 8, NZ), f32),
                pltpu.VMEM((2, 2, 9 * CY, NZ), f32), pltpu.VMEM((2, 2, 48, NZ), f32),
                pltpu.VMEM((2, 2, 2, 24, NZ), f32), pltpu.VMEM((2, 3, 2, 16, NZ), f32),
                pltpu.VMEM((2, 3, 2, 2, 8, NZ), f32), pltpu.VMEM((3 * 2 * ER, NZ), f32),
                pltpu.SemaphoreType.DMA((ROUNDS, 6)), pltpu.SemaphoreType.DMA((ROUNDS, 6)),
                pltpu.SemaphoreType.DMA((SCHUR_ITERS, slots)), pltpu.SemaphoreType.DMA((SCHUR_ITERS, slots)),
                pltpu.SemaphoreType.DMA((2, 26)), pltpu.SemaphoreType.DMA((2, 26)),
            ],
            compiler_params=pltpu.CompilerParams(collective_id=0, has_side_effects=True),
        )(heat, motion, dual, rheology, stiffness)
        return pl.pallas_call(outputs, out_shape=found, in_specs=[vmem] * 4, out_specs=(vmem,) * 3)(*parts)

    return jax.shard_map(
        shards,
        mesh=mesh,
        in_specs=(P(*AXES), P(None, *AXES), P(*AXES), P(*AXES), P()),
        out_specs=(P(*AXES), P(None, *AXES), P(*AXES)),
        check_vma=False,
    )
```
